128 devices in a mesh: row: 16 (over x, z_hi, core), col: 8 (over z_lo, y).
Axes of the slice: x: 4, y: 4, z: 4 (z_hi: 2, z_lo: 2; z = z_hi * 2 + z_lo), core: 2. Of those that a mesh axis runs over, the one named last changes fastest.
Arguments:
- ctrl_start: float32 [65536, 512], P(('row', 'col')), may hold values from -6 to 6
- obsv_start: float32 [65536, 512], P(('row', 'col')), may hold values from -6 to 6
- band_tiles: float32 [65536, 384], P(('row', 'col')), may hold values from -0.15625 to 0.15625
- band_offsets: int32 [512, 3], P(('row', 'col')), may hold values from -2 to 2, as said below
Outputs:
- cross_product: float32 [2048, 2048], P('row', 'col')
The draws below stay inside these ranges and needn't reach their ends.
Inputs may be any that keep to these rules, and one draw needn't show every extreme that they name: `band_offsets`: the 3 offsets of a tile row are distinct.
All inputs are finite; a program needn't handle non-finite values.
Results may differ from the reference program's by a relative error of at most 0.0003.
Values sent between devices are 32-bit elements; how exact they have to be, the bound alone decides.
A program may use at most 128 MiB of HBM per device.

```python
import math
import jax
import jax.numpy as jnp
from jax import lax

TILE = 128
HALO = 2
BAND = 3
INIT_COLS = 512
ORDER = 65536
NTILES = 512


def draw_band_offsets(key, part):
    width = 2 * HALO + 1
    scores = jax.random.randint(jax.random.fold_in(key, 17), (NTILES, width), 0, 1 << 20) * 8 + jnp.arange(width, dtype=jnp.int32)
    picked = jnp.argsort(scores, axis=1)[:, :BAND]
    return (picked - HALO).astype(jnp.int32)


def level_of(key, shape, split, smallest, largest):
    loudness, own = 1.0, jax.random.fold_in(key, 6)
    for position, blocks in split:
        heights = jnp.exp(jax.random.uniform(jax.random.fold_in(own, position), (blocks,), jnp.float32, smallest / len(split), largest / len(split)))
        loudness = loudness * jnp.repeat(heights, shape[position] // blocks).reshape([-1 if axis == position else 1 for axis in range(len(shape))])
    return loudness


def gaussian(key, dims, spread, limit, cuts=(), kind=jnp.bfloat16):
    gain = level_of(key, dims, cuts, -0.22, 0.18) if cuts else 1.0
    entries = jax.random.normal(key, dims, jnp.float32) * spread * gain
    return jnp.minimum(jnp.maximum(entries, -limit), limit).astype(kind)


def setup_inputs(seed: int = 0) -> dict:
    key_of = jax.random.split(jax.random.key(seed), 5)
    return {
        "ctrl_start": gaussian(key_of[0], (ORDER, INIT_COLS), 1.0, 6.0, ((0, 128),), jnp.float32),
        "obsv_start": gaussian(key_of[1], (ORDER, INIT_COLS), 1.0, 6.0, ((0, 128),), jnp.float32),
        "band_tiles": gaussian(key_of[2], (ORDER, BAND * TILE), (4 * BAND * TILE) ** -0.5, 0.15625, ((0, 128),), jnp.float32),
        "band_offsets": draw_band_offsets(jax.random.fold_in(key_of[4], 71), 0),
    }


def forward(field, tiles, offsets):
    count = field.shape[0] // TILE
    margin = HALO * TILE
    padded = jnp.pad(field, ((margin, margin), (0, 0)))

    def one_row(index):
        parts = []
        for slot in range(BAND):
            start = ((index + offsets[index, slot]) * TILE + margin).astype(jnp.int32)
            parts.append(lax.dynamic_slice_in_dim(padded, start, TILE, 0))
        stacked = jnp.concatenate(parts, 0)
        tile_row = lax.dynamic_slice_in_dim(tiles, (index * TILE).astype(jnp.int32), TILE, 0)
        return jnp.dot(tile_row, stacked, precision=lax.Precision.HIGHEST, preferred_element_type=jnp.float32)
    result = lax.map(one_row, jnp.arange(count, dtype=jnp.int32))
    return result.reshape(field.shape[0], field.shape[1])

def transpose(field, tiles, offsets):
    total = field.shape[0]
    count = total // TILE
    margin = HALO * TILE
    padded = jnp.zeros((total + 2 * margin, field.shape[1]), jnp.float32)

    def step(index, acc):
        index = jnp.asarray(index).astype(jnp.int32)
        piece = lax.dynamic_slice_in_dim(field, index * TILE, TILE, 0)
        tile_row = lax.dynamic_slice_in_dim(tiles, index * TILE, TILE, 0)
        terms = jnp.dot(tile_row.T, piece, precision=lax.Precision.HIGHEST, preferred_element_type=jnp.float32)
        for slot in range(BAND):
            start = ((index + offsets[index, slot]) * TILE + margin).astype(jnp.int32)
            current = lax.dynamic_slice_in_dim(acc, start, TILE, 0)
            acc = lax.dynamic_update_slice_in_dim(acc, current + terms[slot * TILE:(slot + 1) * TILE], start, 0)
        return acc
    padded = lax.fori_loop(0, count, step, padded)
    return padded[margin:margin + total]

def reference(ctrl_start, obsv_start, band_tiles, band_offsets):
    ctrl_one = jnp.concatenate([ctrl_start, forward(ctrl_start, band_tiles, band_offsets)], 1)
    ctrl_two = jnp.concatenate([ctrl_one, forward(forward(ctrl_one, band_tiles, band_offsets), band_tiles, band_offsets)], 1)
    obsv_one = jnp.concatenate([obsv_start, transpose(obsv_start, band_tiles, band_offsets)], 1)
    obsv_two = jnp.concatenate([obsv_one, transpose(transpose(obsv_one, band_tiles, band_offsets), band_tiles, band_offsets)], 1)
    product = jnp.dot(obsv_two.T, ctrl_two, precision=lax.Precision.HIGHEST, preferred_element_type=jnp.float32)
    return product * (1.0 / math.sqrt(ORDER))
```

```python
import math

import jax
import jax.numpy as jnp
from jax import lax
from jax.sharding import Mesh
from jax.sharding import PartitionSpec as P

TILE = 128
HALO = 2
BAND = 3
ROW = ("x", "z_hi", "core")
COL = ("z_lo", "y_hi", "y_lo")
ROW_COL = ROW + COL


def extended(array, sides, width):
    for axis, dim in sides:
        size, length = (lax.axis_size(axis), array.shape[dim])
        up = [(i, (i + 1) % size) for i in range(size - 1)]
        down = [(j, i) for i, j in up]
        last = lax.slice_in_dim(array, length - width, length, axis=dim)
        initial = lax.slice_in_dim(array, 0, width, axis=dim)
        before = lax.ppermute(last, axis, up)
        after = lax.ppermute(initial, axis, down)
        array = jnp.concatenate([before, array, after], axis=dim)
    return array


def passed_along(array, axis, by):
    size = lax.axis_size(axis)
    pairs = [(i, i + by) for i in range(size) if 0 <= i + by < size]
    return lax.ppermute(array, axis, pairs)


def forward(field, tiles, offsets):
    margin = HALO * TILE
    padded = extended(field, ((ROW_COL, 0),), margin)
    results = []
    for index in range(field.shape[0] // TILE):
        parts = []
        for slot in range(BAND):
            start = (index + offsets[index, slot]) * TILE + margin
            parts.append(lax.dynamic_slice_in_dim(padded, start, TILE, 0))
        stacked = jnp.concatenate(parts, 0)
        results.append(
            jnp.dot(
                tiles[index * TILE : (index + 1) * TILE],
                stacked,
                precision=lax.Precision.HIGH,
                preferred_element_type=jnp.float32,
            )
        )
    return jnp.concatenate(results, 0)


def transpose(field, tiles, offsets):
    total = field.shape[0]
    margin = HALO * TILE
    padded = jnp.zeros((total + 2 * margin, field.shape[1]), jnp.float32)
    for index in range(total // TILE):
        piece = field[index * TILE : (index + 1) * TILE]
        terms = jnp.dot(
            tiles[index * TILE : (index + 1) * TILE].T,
            piece,
            precision=lax.Precision.HIGH,
            preferred_element_type=jnp.float32,
        )
        for slot in range(BAND):
            start = (index + offsets[index, slot]) * TILE + margin
            current = lax.dynamic_slice_in_dim(padded, start, TILE, 0)
            padded = lax.dynamic_update_slice_in_dim(
                padded, current + terms[slot * TILE : (slot + 1) * TILE], start, 0
            )
    lower = padded[:margin]
    upper = padded[total + margin :]
    middle = padded[margin : total + margin]
    from_above = passed_along(lower, ROW_COL, -1)
    from_below = passed_along(upper, ROW_COL, 1)
    middle = middle.at[:margin].add(from_below)
    middle = middle.at[total - margin :].add(from_above)
    return middle


def hankel(left, right):
    product = jnp.dot(
        left.T, right, precision=lax.Precision.HIGH, preferred_element_type=jnp.float32
    )
    size = product.shape[0] // 4
    half = product.shape[1] // 2
    return product.reshape(4, size, 2, half).transpose(0, 2, 1, 3)


def local(ctrl_start, obsv_start, band_tiles, band_offsets):
    ctrl = [ctrl_start]
    obsv = [obsv_start]
    for step in range(3):
        ctrl.append(forward(ctrl[step], band_tiles, band_offsets))
        obsv.append(transpose(obsv[step], band_tiles, band_offsets))
    blocks = [hankel(obsv[k // 2], ctrl[k - k // 2]) for k in range(7)]
    tiles = jnp.stack(blocks, 0)
    tiles = tiles.reshape(7, 2, 2, 2, *tiles.shape[3:])
    tiles = tiles.transpose(2, 1, 3, 0, 4, 5)
    mine = lax.psum_scatter(tiles, "core", scatter_dimension=0, tiled=True)[0]
    mine = mine.reshape(4, *mine.shape[2:])
    mine = lax.psum_scatter(mine, ("z_hi", "y_lo"), scatter_dimension=0, tiled=True)[0]
    wanted = [x + 2 * z + y for x in range(4) for z in range(2) for y in range(2)]
    spread = jnp.stack([mine[k] for k in wanted], 0)
    block = lax.psum_scatter(spread, ("x", "z_lo", "y_hi"), scatter_dimension=0, tiled=True)[0]
    return block * (1.0 / math.sqrt(ctrl_start.shape[0] * lax.axis_size(ROW_COL)))


def solution(mesh):
    finer = Mesh(mesh.devices.reshape(4, 2, 2, 2, 2, 2), ROW_COL)
    placed = P(ROW_COL, None)
    return jax.shard_map(
        local,
        mesh=finer,
        in_specs=(placed,) * 4,
        out_specs=P(ROW, COL),
        check_vma=False,
    )
```

```python
import math

import jax
import jax.numpy as jnp
from jax import lax
from jax.experimental import pallas as pl
from jax.experimental.pallas import tpu as pltpu
from jax.sharding import PartitionSpec as P

TILE = 128
HALF = 256
ROWS = 512
COLS = 512
ORDER = 65536
BLOCKS = 7
PIECE = 16
MESH = pl.DeviceIdType.MESH
F32 = jnp.float32
BF16 = jnp.bfloat16


def split(value):
    high = value.astype(BF16)
    return high, (value - high.astype(F32)).astype(BF16)


def product(left, right):
    def dot(a, b):
        return jnp.dot(a, b, preferred_element_type=F32)

    return dot(left[0], right[0]) + (dot(left[0], right[1]) + dot(left[1], right[0]))


def kernel(
    ctrl, obsv, band, offsets, out,
    halo_c, halo_o, sent_c, sent_o, part_c, part_o,
    mid_hi, mid_lo, edge_hi, edge_lo, c_hi, c_lo, o_hi, o_lo,
    sent_a, own, got_a, sent_b, got_b, sent_y, got_y, done, got_d,
    hc_send, hc_recv, ho_send, ho_recv, a_send, a_recv, b_send, b_recv, y_send, y_recv, d_sems,
):
    row, col = lax.axis_index("row"), lax.axis_index("col")
    shard = row * 8 + col
    core, z_hi, x = lax.rem(row, 2), lax.rem(lax.div(row, 2), 2), lax.div(row, 4)
    y, z_lo = lax.rem(col, 4), lax.div(col, 4)
    place = x * 4 + z_hi * 2 + z_lo
    before, after = lax.rem(shard + 127, 128), lax.rem(shard + 1, 128)
    before = (lax.div(before, 8), lax.rem(before, 8))
    after = (lax.div(after, 8), lax.rem(after, 8))
    partner = (row + 1 - 2 * core, col)

    def in_plane(d):
        there = lax.rem(place + d, 16)
        xd, zhd, zld = lax.div(there, 4), lax.rem(lax.div(there, 2), 2), lax.rem(there, 2)
        return (xd * 4 + zhd * 2 + core, zld * 4 + y), zhd * TILE + (xd * 2 + zld) * PIECE

    def along_y(d):
        yd = lax.rem(y + d, 4)
        return (row, z_lo * 4 + yd), lax.rem(yd, 2)

    barrier = pltpu.get_barrier_semaphore()
    for device in (before, after, partner):
        pl.semaphore_signal(barrier, inc=1, device_id=device, device_id_type=MESH)

    def greet_plane(d, carry):
        pl.semaphore_signal(barrier, inc=1, device_id=in_plane(d)[0], device_id_type=MESH)
        return carry

    def greet_y(d, carry):
        pl.semaphore_signal(barrier, inc=1, device_id=along_y(d)[0], device_id_type=MESH)
        return carry

    lax.fori_loop(1, 16, greet_plane, 0)
    lax.fori_loop(1, 4, greet_y, 0)
    pl.semaphore_wait(barrier, 21)

    def remote(source, target, send, recv, device):
        return pltpu.make_async_remote_copy(
            src_ref=source,
            dst_ref=target,
            send_sem=send,
            recv_sem=recv,
            device_id=device,
            device_id_type=MESH,
        )

    def exchange(halves, halo, send, recv, k):
        copies = (
            remote(halves[0], halo.at[k, 1], send.at[k, 0], recv.at[k, 1], before),
            remote(halves[1], halo.at[k, 0], send.at[k, 1], recv.at[k, 0], after),
        )
        return copies

    def wait_all(ref, semaphore):
        pltpu.make_async_copy(ref, ref, semaphore).wait()

    c_copies = [
        exchange((src.at[pl.ds(0, HALF)], src.at[pl.ds(HALF, HALF)]), halo_c, hc_send, hc_recv, k)
        for k, src in enumerate((ctrl, sent_c.at[0], sent_c.at[1]))
    ]
    o_copies = [
        exchange((sent_o.at[k, 0], sent_o.at[k, 1]), halo_o, ho_send, ho_recv, k)
        for k in range(3)
    ]
    for copy in c_copies[0]:
        copy.start()

    mid_hi[...] = jnp.zeros_like(mid_hi)
    mid_lo[...] = jnp.zeros_like(mid_lo)
    edge_hi[...] = jnp.zeros_like(edge_hi)
    edge_lo[...] = jnp.zeros_like(edge_lo)
    no_before = 1 - lax.min(shard, 1)
    no_after = lax.div(shard, 127)
    for t in range(4):
        tiles = [band[pl.ds(t * TILE, TILE), pl.ds(b * TILE, TILE)] for b in range(3)]
        for o in range(5):
            e = t + o
            tile = jnp.zeros((TILE, TILE), F32)
            for b in range(3):
                given = offsets[t, b]
                if e < 2:
                    given = given + 100 * no_before
                if e >= 6:
                    given = given + 100 * no_after
                tile = jnp.where(jnp.full((TILE, TILE), given, jnp.int32) == o - 2, tiles[b], tile)
            high, low = split(tile)
            if e < 2:
                to_hi, to_lo, r, c = edge_hi.at[0], edge_lo.at[0], t, e
            elif e < 6:
                to_hi, to_lo, r, c = mid_hi, mid_lo, t, e - 2
            else:
                to_hi, to_lo, r, c = edge_hi.at[1], edge_lo.at[1], t - 2, e - 6
            to_hi[pl.ds(r * TILE, TILE), pl.ds(c * TILE, TILE)] = high
            to_lo[pl.ds(r * TILE, TILE), pl.ds(c * TILE, TILE)] = low

    for q in range(4):
        high, low = split(obsv[:, pl.ds(q * TILE, TILE)].T)
        at = pl.ds((q % 2) * HALF + (q // 2) * TILE, TILE)
        o_hi[at, :] = high
        o_lo[at, :] = low
    c_hi[...], c_lo[...] = split(ctrl[...])

    def send_o(k):
        for h in range(2):
            at = pl.ds(h * HALF, HALF)
            sent_o[k, h] = product((o_hi[:, at], o_lo[:, at]), (edge_hi[h], edge_lo[h]))
            o_copies[k][h].start()

    def mid_o():
        for h in range(2):
            at = pl.ds(h * HALF, HALF)
            part_o[:, at] = product((o_hi[...], o_lo[...]), (mid_hi[:, at], mid_lo[:, at]))

    def mid_c():
        for h in range(2):
            at = pl.ds(h * HALF, HALF)
            part_c[:, at] = product((mid_hi[...], mid_lo[...]), (c_hi[:, at], c_lo[:, at]))

    def next_c(k):
        for h in range(2):
            c_copies[k][1 - h].wait_recv()
            at = pl.ds(h * HALF, HALF)
            value = part_c[at, :] + product((edge_hi[h], edge_lo[h]), split(halo_c[k, h]))
            if k < 2:
                sent_c[k, at, :] = value
                c_copies[k + 1][h].start()
            c_hi[at, :], c_lo[at, :] = split(value)

    def next_o(k):
        for h in range(2):
            o_copies[k][1 - h].wait_recv()
            at = pl.ds(h * HALF, HALF)
            o_hi[:, at], o_lo[:, at] = split(part_o[:, at] + halo_o[k, h])

    def a_copy(k):
        return remote(sent_a.at[k], got_a.at[k], a_send.at[k], a_recv.at[k], partner)

    def block(k):
        def rows_of(which):
            at = pl.ds(pl.multiple_of(which * HALF, HALF), HALF)
            return product((o_hi[at, :], o_lo[at, :]), (c_hi[...], c_lo[...]))

        sent_a[k] = rows_of(1 - core)
        a_copy(k).start()
        own[...] = rows_of(core)

    def plane(k):
        a_copy(k).wait_recv()
        sent_b[k] = own[...] + got_a[k]

        def send(d, carry):
            device, at = in_plane(d)
            remote(
                sent_b.at[k, pl.ds(pl.multiple_of(at, PIECE), PIECE)],
                got_b.at[k, 15 - d],
                b_send.at[k],
                b_recv.at[k],
                device,
            ).start()
            return carry

        lax.fori_loop(1, 16, send, 0)

    def over_y(k):
        wait_all(got_b.at[k], b_recv.at[k])
        at = pl.multiple_of(z_hi * TILE + (x * 2 + z_lo) * PIECE, PIECE)
        total = sent_b[k, pl.ds(at, PIECE), :]
        for i in range(15):
            total = total + got_b[k, i]
        sent_y[k, 0] = total[:, :HALF]
        sent_y[k, 1] = total[:, HALF:]

        def send(d, carry):
            device, half = along_y(d)
            remote(
                sent_y.at[k, half], got_y.at[k, 3 - d], y_send.at[k], y_recv.at[k], device
            ).start()
            return carry

        lax.fori_loop(1, 4, send, 0)

    def finish(k):
        wait_all(got_y.at[k], y_recv.at[k])
        total = sent_y[k, lax.rem(y, 2)] + got_y[k, 0] + got_y[k, 1] + got_y[k, 2]
        done[k] = total * (1.0 / math.sqrt(ORDER))

    send_o(0)
    mid_o()
    block(0)
    mid_c()
    plane(0)

    next_c(0)
    block(1)
    mid_c()
    plane(1)
    over_y(0)

    next_o(0)
    send_o(1)
    block(2)
    mid_o()
    plane(2)
    over_y(1)
    finish(0)

    next_c(1)
    block(3)
    mid_c()
    plane(3)
    over_y(2)
    finish(1)

    next_o(1)
    send_o(2)
    block(4)
    mid_o()
    plane(4)
    over_y(3)
    finish(2)

    next_c(2)
    block(5)
    plane(5)
    over_y(4)
    finish(3)

    next_o(2)
    block(6)
    plane(6)
    over_y(5)
    finish(4)
    over_y(6)
    finish(5)
    finish(6)

    mine = x * 2 + z_lo

    def send_done(d, carry):
        there = lax.rem(mine + d, 8)
        xd, zld = lax.div(there, 2), lax.rem(there, 2)
        remote(
            done.at[xd + 2 * zld + lax.div(y, 2)],
            got_d.at[7 - d],
            d_sems.at[0],
            d_sems.at[1],
            (xd * 4 + z_hi * 2 + core, zld * 4 + y),
        ).start()
        return carry

    lax.fori_loop(1, 8, send_done, 0)
    out[pl.ds(pl.multiple_of(mine * PIECE, PIECE), PIECE), :] = done[
        x + 2 * z_lo + lax.div(y, 2)
    ]
    wait_all(got_d, d_sems.at[1])
    for i in range(7):
        source = lax.rem(mine + 1 + i, 8)
        out[pl.ds(pl.multiple_of(source * PIECE, PIECE), PIECE), :] = got_d[i]

    wait_all(got_d, d_sems.at[0])
    for copies in c_copies + o_copies:
        for copy in copies:
            copy.wait_send()
    for k in range(BLOCKS):
        a_copy(k).wait_send()
        wait_all(got_b.at[k], b_send.at[k])
        wait_all(got_y.at[k], y_send.at[k])


def local(ctrl_start, obsv_start, band_tiles, band_offsets):
    vmem, dma = pltpu.VMEM, pltpu.SemaphoreType.DMA
    return pl.pallas_call(
        kernel,
        out_shape=jax.ShapeDtypeStruct((TILE, HALF), F32),
        in_specs=[pl.BlockSpec(memory_space=pltpu.VMEM)] * 3
        + [pl.BlockSpec(memory_space=pltpu.SMEM)],
        out_specs=pl.BlockSpec(memory_space=pltpu.VMEM),
        scratch_shapes=[
            vmem((3, 2, HALF, COLS), F32),
            vmem((3, 2, COLS, HALF), F32),
            vmem((2, ROWS, COLS), F32),
            vmem((3, 2, COLS, HALF), F32),
            vmem((ROWS, COLS), F32),
            vmem((COLS, ROWS), F32),
            vmem((ROWS, ROWS), BF16),
            vmem((ROWS, ROWS), BF16),
            vmem((2, HALF, HALF), BF16),
            vmem((2, HALF, HALF), BF16),
            vmem((ROWS, COLS), BF16),
            vmem((ROWS, COLS), BF16),
            vmem((COLS, ROWS), BF16),
            vmem((COLS, ROWS), BF16),
            vmem((BLOCKS, HALF, COLS), F32),
            vmem((HALF, COLS), F32),
            vmem((BLOCKS, HALF, COLS), F32),
            vmem((BLOCKS, HALF, COLS), F32),
            vmem((BLOCKS, 15, PIECE, COLS), F32),
            vmem((BLOCKS, 2, PIECE, HALF), F32),
            vmem((BLOCKS, 3, PIECE, HALF), F32),
            vmem((BLOCKS, PIECE, HALF), F32),
            vmem((7, PIECE, HALF), F32),
            dma((3, 2)),
            dma((3, 2)),
            dma((3, 2)),
            dma((3, 2)),
            dma((BLOCKS,)),
            dma((BLOCKS,)),
            dma((BLOCKS,)),
            dma((BLOCKS,)),
            dma((BLOCKS,)),
            dma((BLOCKS,)),
            dma((2,)),
        ],
        compiler_params=pltpu.CompilerParams(
            collective_id=0, has_side_effects=True, vmem_limit_bytes=60 * 1024 * 1024
        ),
    )(ctrl_start, obsv_start, band_tiles, band_offsets)


def solution(mesh):
    placed = P(("row", "col"), None)
    return jax.shard_map(
        local, mesh=mesh, in_specs=(placed,) * 4, out_specs=P("row", "col"), check_vma=False
    )
```

```python
import math

import jax
import jax.numpy as jnp
from jax import lax
from jax.experimental import pallas as pl
from jax.experimental.pallas import tpu as pltpu
from jax.sharding import PartitionSpec as P

TILE = 128
HALF = 256
ROWS = 512
COLS = 512
ORDER = 65536
BLOCKS = 7
PIECE = 16
MESH = pl.DeviceIdType.MESH
F32 = jnp.float32
BF16 = jnp.bfloat16


def split(value):
    high = value.astype(BF16)
    return high, (value - high.astype(F32)).astype(BF16)


def product(left, right):
    def dot(a, b):
        return jnp.dot(a, b, preferred_element_type=F32)

    return dot(left[0], right[0]) + (dot(left[0], right[1]) + dot(left[1], right[0]))


def kernel(
    ctrl_in, obsv_in, band_in, offsets, out, ctrl, obsv, band,
    halo_c, halo_o, sent_c, sent_o, part_c, part_o,
    mid_hi, mid_lo, edge_hi, edge_lo, c_hi, c_lo, o_hi, o_lo,
    sent_a, own, got_a, sent_x, got_x, sent_z, got_z, got_p, sent_y, got_y, done, got_d,
    in_sems, hc_send, hc_recv, ho_send, ho_recv, last_send, last_recv, a_send, a_recv,
    x_send, x_recv, z_send, z_recv, p_sems, y_send, y_recv, d_sems,
):
    row, col = lax.axis_index("row"), lax.axis_index("col")
    shard = row * 8 + col
    core, z_hi, x = lax.rem(row, 2), lax.rem(lax.div(row, 2), 2), lax.div(row, 4)
    y, z_lo = lax.rem(col, 4), lax.div(col, 4)
    place = x * 4 + z_hi * 2 + z_lo
    mine = x * 2 + z_lo
    y_hi = lax.div(y, 2)
    before, after = lax.rem(shard + 127, 128), lax.rem(shard + 1, 128)
    before = (lax.div(before, 8), lax.rem(before, 8))
    after = (lax.div(after, 8), lax.rem(after, 8))
    partner = (row + 1 - 2 * core, col)

    def in_plane(d):
        there = lax.rem(place + d, 16)
        xd, zhd, zld = lax.div(there, 4), lax.rem(lax.div(there, 2), 2), lax.rem(there, 2)
        return xd * 4 + zhd * 2 + core, zld * 4 + y

    def along_y(d):
        yd = lax.rem(y + d, 4)
        return (row, z_lo * 4 + yd), lax.rem(yd, 2)

    barrier = pltpu.get_barrier_semaphore()
    for device in (before, after, partner):
        pl.semaphore_signal(barrier, inc=1, device_id=device, device_id_type=MESH)

    def greet_plane(d, carry):
        pl.semaphore_signal(barrier, inc=1, device_id=in_plane(d), device_id_type=MESH)
        return carry

    def greet_y(d, carry):
        pl.semaphore_signal(barrier, inc=1, device_id=along_y(d)[0], device_id_type=MESH)
        return carry

    lax.fori_loop(1, 16, greet_plane, 0)
    lax.fori_loop(1, 4, greet_y, 0)
    inputs = [
        pltpu.make_async_copy(source, target, in_sems.at[i])
        for i, (source, target) in enumerate(((band_in, band), (obsv_in, obsv), (ctrl_in, ctrl)))
    ]
    for copy in inputs:
        copy.start()
    pl.semaphore_wait(barrier, 21)

    def remote(source, target, send, recv, device):
        return pltpu.make_async_remote_copy(
            src_ref=source,
            dst_ref=target,
            send_sem=send,
            recv_sem=recv,
            device_id=device,
            device_id_type=MESH,
        )

    def exchange(halves, halo, send, recv, k):
        copies = (
            remote(halves[0], halo.at[k, 1], send.at[k, 0], recv.at[k, 1], before),
            remote(halves[1], halo.at[k, 0], send.at[k, 1], recv.at[k, 0], after),
        )
        return copies

    def wait_all(ref, semaphore):
        pltpu.make_async_copy(ref, ref, semaphore).wait()

    c_copies = [
        exchange((src.at[pl.ds(0, HALF)], src.at[pl.ds(HALF, HALF)]), halo_c, hc_send, hc_recv, k)
        for k, src in enumerate((ctrl_in, sent_c.at[0], sent_c.at[1]))
    ]
    o_copies = [
        exchange((sent_o.at[k, 0], sent_o.at[k, 1]), halo_o, ho_send, ho_recv, k)
        for k in range(2)
    ]

    def last_copy(side, chunk):
        return remote(
            sent_o.at[2, side, pl.ds(pl.multiple_of(chunk * TILE, TILE), TILE)],
            halo_o.at[2, 1 - side, pl.ds(pl.multiple_of(chunk * TILE, TILE), TILE)],
            last_send.at[side, chunk],
            last_recv.at[1 - side, chunk],
            (before, after)[side],
        )

    for copy in c_copies[0]:
        copy.start()

    inputs[0].wait()
    mid_hi[...] = jnp.zeros_like(mid_hi)
    mid_lo[...] = jnp.zeros_like(mid_lo)
    edge_hi[...] = jnp.zeros_like(edge_hi)
    edge_lo[...] = jnp.zeros_like(edge_lo)
    no_before = 1 - lax.min(shard, 1)
    no_after = lax.div(shard, 127)
    for t in range(4):
        tiles = [band[pl.ds(t * TILE, TILE), pl.ds(b * TILE, TILE)] for b in range(3)]
        for o in range(5):
            e = t + o
            tile = jnp.zeros((TILE, TILE), F32)
            for b in range(3):
                given = offsets[t, b]
                if e < 2:
                    given = given + 100 * no_before
                if e >= 6:
                    given = given + 100 * no_after
                tile = jnp.where(jnp.full((TILE, TILE), given, jnp.int32) == o - 2, tiles[b], tile)
            high, low = split(tile)
            if e < 2:
                to_hi, to_lo, r, c = edge_hi.at[0], edge_lo.at[0], t, e
            elif e < 6:
                to_hi, to_lo, r, c = mid_hi, mid_lo, t, e - 2
            else:
                to_hi, to_lo, r, c = edge_hi.at[1], edge_lo.at[1], t - 2, e - 6
            to_hi[pl.ds(r * TILE, TILE), pl.ds(c * TILE, TILE)] = high
            to_lo[pl.ds(r * TILE, TILE), pl.ds(c * TILE, TILE)] = low

    inputs[1].wait()
    for q in range(4):
        high, low = split(obsv[:, pl.ds(q * TILE, TILE)].T)
        at = pl.ds((q % 2) * HALF + (q // 2) * TILE, TILE)
        o_hi[at, :] = high
        o_lo[at, :] = low
    inputs[2].wait()
    c_hi[...], c_lo[...] = split(ctrl[...])

    def send_o(k):
        for h in range(2):
            at = pl.ds(h * HALF, HALF)
            sent_o[k, h] = product((o_hi[:, at], o_lo[:, at]), (edge_hi[h], edge_lo[h]))
            o_copies[k][h].start()

    def chunks_for(its_core):
        return [(1 - its_core) * 2, (1 - its_core) * 2 + 1, its_core * 2, its_core * 2 + 1]

    def rows(chunk):
        return pl.ds(pl.multiple_of(chunk * TILE, TILE), TILE)

    def send_last_o():
        orders = [chunks_for(lax.rem(device[0], 2)) for device in (before, after)]
        for i in range(4):
            for h in range(2):
                at = rows(orders[h][i])
                columns = pl.ds(h * HALF, HALF)
                sent_o[2, h, at, :] = product(
                    (o_hi[at, columns], o_lo[at, columns]), (edge_hi[h], edge_lo[h])
                )
                last_copy(h, orders[h][i]).start()

    def last_rows(chunk):
        at = rows(chunk)
        for h in range(2):
            last_copy(1 - h, chunk).wait_recv()
            columns = pl.ds(h * HALF, HALF)
            o_hi[at, columns], o_lo[at, columns] = split(
                part_o[at, columns] + halo_o[2, h, at, :]
            )
        return product((o_hi[at, :], o_lo[at, :]), (c_hi[...], c_lo[...]))

    def mid_o():
        for h in range(2):
            at = pl.ds(h * HALF, HALF)
            part_o[:, at] = product((o_hi[...], o_lo[...]), (mid_hi[:, at], mid_lo[:, at]))

    def mid_c():
        for h in range(2):
            at = pl.ds(h * HALF, HALF)
            part_c[:, at] = product((mid_hi[...], mid_lo[...]), (c_hi[:, at], c_lo[:, at]))

    def next_c(k):
        for h in range(2):
            c_copies[k][1 - h].wait_recv()
            at = pl.ds(h * HALF, HALF)
            value = part_c[at, :] + product((edge_hi[h], edge_lo[h]), split(halo_c[k, h]))
            if k < 2:
                sent_c[k, at, :] = value
                c_copies[k + 1][h].start()
            c_hi[at, :], c_lo[at, :] = split(value)

    def next_o(k):
        for h in range(2):
            o_copies[k][1 - h].wait_recv()
            at = pl.ds(h * HALF, HALF)
            o_hi[:, at], o_lo[:, at] = split(part_o[:, at] + halo_o[k, h])

    def a_copy(k, z):
        at = pl.ds(z * TILE, TILE)
        return remote(
            sent_a.at[k, at], got_a.at[k, at], a_send.at[k, z], a_recv.at[k, z], partner
        )

    def block(k):
        def rows_of(which):
            at = pl.ds(pl.multiple_of(which * HALF, HALF), HALF)
            return product((o_hi[at, :], o_lo[at, :]), (c_hi[...], c_lo[...]))

        sent_a[k] = rows_of(1 - core)
        for z in range(2):
            a_copy(k, z).start()
        own[...] = rows_of(core)

    def over_x(k):
        for z in range(2):
            a_copy(k, z).wait_recv()
        sent_x[k] = (own[...] + got_a[k]).reshape(2, 4, 2 * PIECE, COLS)

        def send(d, carry):
            xd = lax.rem(x + d, 4)
            remote(
                sent_x.at[k, :, xd],
                got_x.at[k, 3 - d],
                x_send.at[k],
                x_recv.at[k],
                (xd * 4 + z_hi * 2 + core, col),
            ).start()
            return carry

        lax.fori_loop(1, 4, send, 0)

    def over_z(k):
        wait_all(got_x.at[k], x_recv.at[k])
        sent_z[k] = sent_x[k, :, x] + got_x[k, 0] + got_x[k, 1] + got_x[k, 2]

        def send(d, carry):
            there = lax.rem(z_hi * 2 + z_lo + d, 4)
            zhd, zld = lax.div(there, 2), lax.rem(there, 2)
            remote(
                sent_z.at[k, zhd, pl.ds(pl.multiple_of(zld * PIECE, PIECE), PIECE)],
                got_z.at[k, 3 - d],
                z_send.at[k],
                z_recv.at[k],
                (x * 4 + zhd * 2 + core, zld * 4 + y),
            ).start()
            return carry

        lax.fori_loop(1, 4, send, 0)

    def send_y(k, total):
        sent_y[k, 0] = total[:, :HALF]
        sent_y[k, 1] = total[:, HALF:]

        def send(d, carry):
            device, half = along_y(d)
            remote(
                sent_y.at[k, half], got_y.at[k, 3 - d], y_send.at[k], y_recv.at[k], device
            ).start()
            return carry

        lax.fori_loop(1, 4, send, 0)

    def over_y(k):
        wait_all(got_z.at[k], z_recv.at[k])
        at = pl.ds(pl.multiple_of(z_lo * PIECE, PIECE), PIECE)
        send_y(k, sent_z[k, z_hi, at, :] + got_z[k, 0] + got_z[k, 1] + got_z[k, 2])

    def last_plane(z):
        same = z_hi if z else 1 - z_hi

        def send(d, carry):
            there = lax.rem(mine + d, 8)
            xd, zld = lax.div(there, 2), lax.rem(there, 2)

            @pl.when(d + 1 - same > 0)
            def _():
                remote(
                    sent_x.at[6, z, xd, pl.ds(pl.multiple_of(zld * PIECE, PIECE), PIECE)],
                    got_p.at[7 + d * (1 - 2 * same)],
                    p_sems.at[0],
                    p_sems.at[1],
                    (xd * 4 + z * 2 + core, zld * 4 + y),
                ).start()

            return carry

        lax.fori_loop(0, 8, send, 0)

    def last_over_y():
        wait_all(got_p, p_sems.at[1])
        total = sent_x[6, z_hi, x, pl.ds(pl.multiple_of(z_lo * PIECE, PIECE), PIECE), :]
        for i in range(15):
            total = total + got_p[i]
        send_y(6, total)

    def finish(k):
        wait_all(got_y.at[k], y_recv.at[k])
        total = sent_y[k, lax.rem(y, 2)] + got_y[k, 0] + got_y[k, 1] + got_y[k, 2]
        done[k] = total * (1.0 / math.sqrt(ORDER))

    def send_done(first, last):
        def send(d, carry):
            there = lax.rem(mine + d, 8)
            xd, zld = lax.div(there, 2), lax.rem(there, 2)
            wanted = xd + 2 * zld + y_hi

            @pl.when(jnp.logical_and(wanted >= first, wanted <= last))
            def _():
                remote(
                    done.at[wanted],
                    got_d.at[7 - d],
                    d_sems.at[0],
                    d_sems.at[1],
                    (xd * 4 + z_hi * 2 + core, zld * 4 + y),
                ).start()

            return carry

        lax.fori_loop(1, 8, send, 0)

    send_o(0)
    mid_o()
    block(0)
    mid_c()
    over_x(0)

    next_c(0)
    block(1)
    mid_c()
    over_x(1)
    over_z(0)

    next_o(0)
    send_o(1)
    block(2)
    mid_o()
    over_x(2)
    over_z(1)
    over_y(0)

    next_c(1)
    block(3)
    mid_c()
    over_x(3)
    over_z(2)
    over_y(1)
    finish(0)

    next_o(1)
    send_last_o()
    block(4)
    mid_o()
    over_x(4)
    over_z(3)
    over_y(2)
    finish(1)

    next_c(2)
    block(5)
    over_x(5)
    over_z(4)
    over_y(3)
    finish(2)

    for z in range(2):
        sent_a[6, pl.ds(z * TILE, TILE), :] = last_rows((1 - core) * 2 + z)
        a_copy(6, z).start()
    over_z(5)
    over_y(4)
    finish(3)
    for z in range(2):
        value = last_rows(core * 2 + z)
        a_copy(6, z).wait_recv()
        sent_x[6, z] = (value + got_a[6, pl.ds(z * TILE, TILE), :]).reshape(4, 2 * PIECE, COLS)
        last_plane(z)
    over_y(5)
    finish(4)
    finish(5)
    send_done(0, 5)
    last_over_y()
    finish(6)
    send_done(6, 6)

    out[pl.ds(pl.multiple_of(mine * PIECE, PIECE), PIECE), :] = done[x + 2 * z_lo + y_hi]
    wait_all(got_d, d_sems.at[1])
    for i in range(7):
        source = lax.rem(mine + 1 + i, 8)
        out[pl.ds(pl.multiple_of(source * PIECE, PIECE), PIECE), :] = got_d[i]

    wait_all(got_d, d_sems.at[0])
    for copies in c_copies + o_copies:
        for copy in copies:
            copy.wait_send()
    for chunk in range(4):
        for side in range(2):
            last_copy(side, chunk).wait_send()
    for k in range(BLOCKS):
        for z in range(2):
            a_copy(k, z).wait_send()
        wait_all(got_y.at[k], y_send.at[k])
        if k < 6:
            wait_all(got_x.at[k], x_send.at[k])
            wait_all(got_z.at[k], z_send.at[k])
    wait_all(got_p, p_sems.at[0])


def local(ctrl_start, obsv_start, band_tiles, band_offsets):
    vmem, dma = pltpu.VMEM, pltpu.SemaphoreType.DMA
    return pl.pallas_call(
        kernel,
        out_shape=jax.ShapeDtypeStruct((TILE, HALF), F32),
        in_specs=[pl.BlockSpec(memory_space=pl.ANY)] * 3
        + [pl.BlockSpec(memory_space=pltpu.SMEM)],
        out_specs=pl.BlockSpec(memory_space=pltpu.VMEM),
        scratch_shapes=[
            vmem((ROWS, COLS), F32),
            vmem((ROWS, COLS), F32),
            vmem((ROWS, 3 * TILE), F32),
            vmem((3, 2, HALF, COLS), F32),
            vmem((3, 2, COLS, HALF), F32),
            vmem((2, ROWS, COLS), F32),
            vmem((3, 2, COLS, HALF), F32),
            vmem((ROWS, COLS), F32),
            vmem((COLS, ROWS), F32),
            vmem((ROWS, ROWS), BF16),
            vmem((ROWS, ROWS), BF16),
            vmem((2, HALF, HALF), BF16),
            vmem((2, HALF, HALF), BF16),
            vmem((ROWS, COLS), BF16),
            vmem((ROWS, COLS), BF16),
            vmem((COLS, ROWS), BF16),
            vmem((COLS, ROWS), BF16),
            vmem((BLOCKS, HALF, COLS), F32),
            vmem((HALF, COLS), F32),
            vmem((BLOCKS, HALF, COLS), F32),
            vmem((BLOCKS, 2, 4, 2 * PIECE, COLS), F32),
            vmem((6, 3, 2, 2 * PIECE, COLS), F32),
            vmem((6, 2, 2 * PIECE, COLS), F32),
            vmem((6, 3, PIECE, COLS), F32),
            vmem((15, PIECE, COLS), F32),
            vmem((BLOCKS, 2, PIECE, HALF), F32),
            vmem((BLOCKS, 3, PIECE, HALF), F32),
            vmem((BLOCKS, PIECE, HALF), F32),
            vmem((7, PIECE, HALF), F32),
            dma((3,)),
            dma((3, 2)),
            dma((3, 2)),
            dma((2, 2)),
            dma((2, 2)),
            dma((2, 4)),
            dma((2, 4)),
            dma((BLOCKS, 2)),
            dma((BLOCKS, 2)),
            dma((6,)),
            dma((6,)),
            dma((6,)),
            dma((6,)),
            dma((2,)),
            dma((BLOCKS,)),
            dma((BLOCKS,)),
            dma((2,)),
        ],
        compiler_params=pltpu.CompilerParams(
            collective_id=0, has_side_effects=True, vmem_limit_bytes=60 * 1024 * 1024
        ),
    )(ctrl_start, obsv_start, band_tiles, band_offsets)


def solution(mesh):
    placed = P(("row", "col"), None)
    return jax.shard_map(
        local, mesh=mesh, in_specs=(placed,) * 4, out_specs=P("row", "col"), check_vma=False
    )
```

```python
import math

import jax
import jax.numpy as jnp
from jax import lax
from jax.experimental import pallas as pl
from jax.experimental.pallas import tpu as pltpu
from jax.sharding import PartitionSpec as P

TILE = 128
HALF = 256
ROWS = 512
COLS = 512
ORDER = 65536
BLOCKS = 7
PIECE = 16
MESH = pl.DeviceIdType.MESH
F32 = jnp.float32
BF16 = jnp.bfloat16


def split(value):
    high = value.astype(BF16)
    return high, (value - high.astype(F32)).astype(BF16)


def product(left, right):
    def dot(a, b):
        return jnp.dot(a, b, preferred_element_type=F32)

    return dot(left[0], right[0]) + (dot(left[0], right[1]) + dot(left[1], right[0]))


def kernel(
    ctrl_in, obsv_in, band_in, offsets, out, ctrl, obsv, band,
    halo_c, halo_o, sent_c, sent_o, part_c, part_o,
    mid_hi, mid_lo, edge_hi, edge_lo, c_hi, c_lo, o_hi, o_lo,
    sent_a, own, got_a, sent_x, got_x, sent_z, ring_z, got_z, got_p, sent_y, got_y, done, got_d,
    in_sems, hc_send, hc_recv, ho_send, ho_recv, last_send, last_recv, a_send, a_recv,
    x_send, x_recv, z_send, z_recv, p_sems, y_send, y_recv, d_sems,
):
    row, col = lax.axis_index("row"), lax.axis_index("col")
    shard = row * 8 + col
    core, z_hi, x = lax.rem(row, 2), lax.rem(lax.div(row, 2), 2), lax.div(row, 4)
    y, z_lo = lax.rem(col, 4), lax.div(col, 4)
    place = x * 4 + z_hi * 2 + z_lo
    mine = x * 2 + z_lo
    y_hi = lax.div(y, 2)
    before, after = lax.rem(shard + 127, 128), lax.rem(shard + 1, 128)
    before = (lax.div(before, 8), lax.rem(before, 8))
    after = (lax.div(after, 8), lax.rem(after, 8))
    partner = (row + 1 - 2 * core, col)

    def in_plane(d):
        there = lax.rem(place + d, 16)
        xd, zhd, zld = lax.div(there, 4), lax.rem(lax.div(there, 2), 2), lax.rem(there, 2)
        return xd * 4 + zhd * 2 + core, zld * 4 + y

    def along_y(d):
        yd = lax.rem(y + d, 4)
        return (row, z_lo * 4 + yd), lax.rem(yd, 2)

    barrier = pltpu.get_barrier_semaphore()
    for device in (before, after, partner):
        pl.semaphore_signal(barrier, inc=1, device_id=device, device_id_type=MESH)

    def greet_plane(d, carry):
        pl.semaphore_signal(barrier, inc=1, device_id=in_plane(d), device_id_type=MESH)
        return carry

    def greet_y(d, carry):
        pl.semaphore_signal(barrier, inc=1, device_id=along_y(d)[0], device_id_type=MESH)
        return carry

    lax.fori_loop(1, 16, greet_plane, 0)
    lax.fori_loop(1, 4, greet_y, 0)
    inputs = [
        pltpu.make_async_copy(source, target, in_sems.at[i])
        for i, (source, target) in enumerate(((band_in, band), (obsv_in, obsv), (ctrl_in, ctrl)))
    ]
    for copy in inputs:
        copy.start()
    pl.semaphore_wait(barrier, 21)

    def remote(source, target, send, recv, device):
        return pltpu.make_async_remote_copy(
            src_ref=source,
            dst_ref=target,
            send_sem=send,
            recv_sem=recv,
            device_id=device,
            device_id_type=MESH,
        )

    def exchange(halves, halo, send, recv, k):
        copies = (
            remote(halves[0], halo.at[k, 1], send.at[k, 0], recv.at[k, 1], before),
            remote(halves[1], halo.at[k, 0], send.at[k, 1], recv.at[k, 0], after),
        )
        return copies

    def wait_all(ref, semaphore):
        pltpu.make_async_copy(ref, ref, semaphore).wait()

    c_copies = [
        exchange((src.at[pl.ds(0, HALF)], src.at[pl.ds(HALF, HALF)]), halo_c, hc_send, hc_recv, k)
        for k, src in enumerate((ctrl_in, sent_c.at[0], sent_c.at[1]))
    ]
    o_copies = [
        exchange((sent_o.at[k, 0], sent_o.at[k, 1]), halo_o, ho_send, ho_recv, k)
        for k in range(2)
    ]

    def last_copy(side, chunk):
        return remote(
            sent_o.at[2, side, pl.ds(pl.multiple_of(chunk * TILE, TILE), TILE)],
            halo_o.at[2, 1 - side, pl.ds(pl.multiple_of(chunk * TILE, TILE), TILE)],
            last_send.at[side, chunk],
            last_recv.at[1 - side, chunk],
            (before, after)[side],
        )

    for copy in c_copies[0]:
        copy.start()

    inputs[0].wait()
    mid_hi[...] = jnp.zeros_like(mid_hi)
    mid_lo[...] = jnp.zeros_like(mid_lo)
    edge_hi[...] = jnp.zeros_like(edge_hi)
    edge_lo[...] = jnp.zeros_like(edge_lo)
    no_before = 1 - lax.min(shard, 1)
    no_after = lax.div(shard, 127)
    for t in range(4):
        tiles = [band[pl.ds(t * TILE, TILE), pl.ds(b * TILE, TILE)] for b in range(3)]
        for o in range(5):
            e = t + o
            tile = jnp.zeros((TILE, TILE), F32)
            for b in range(3):
                given = offsets[t, b]
                if e < 2:
                    given = given + 100 * no_before
                if e >= 6:
                    given = given + 100 * no_after
                tile = jnp.where(jnp.full((TILE, TILE), given, jnp.int32) == o - 2, tiles[b], tile)
            high, low = split(tile)
            if e < 2:
                to_hi, to_lo, r, c = edge_hi.at[0], edge_lo.at[0], t, e
            elif e < 6:
                to_hi, to_lo, r, c = mid_hi, mid_lo, t, e - 2
            else:
                to_hi, to_lo, r, c = edge_hi.at[1], edge_lo.at[1], t - 2, e - 6
            to_hi[pl.ds(r * TILE, TILE), pl.ds(c * TILE, TILE)] = high
            to_lo[pl.ds(r * TILE, TILE), pl.ds(c * TILE, TILE)] = low

    inputs[1].wait()
    for q in range(4):
        high, low = split(obsv[:, pl.ds(q * TILE, TILE)].T)
        at = pl.ds((q % 2) * HALF + (q // 2) * TILE, TILE)
        o_hi[at, :] = high
        o_lo[at, :] = low
    inputs[2].wait()
    c_hi[...], c_lo[...] = split(ctrl[...])

    def send_o(k):
        for h in range(2):
            at = pl.ds(h * HALF, HALF)
            sent_o[k, h] = product((o_hi[:, at], o_lo[:, at]), (edge_hi[h], edge_lo[h]))
            o_copies[k][h].start()

    def chunks_for(its_core):
        return [(1 - its_core) * 2, (1 - its_core) * 2 + 1, its_core * 2, its_core * 2 + 1]

    def rows(chunk):
        return pl.ds(pl.multiple_of(chunk * TILE, TILE), TILE)

    def send_last_o():
        orders = [chunks_for(lax.rem(device[0], 2)) for device in (before, after)]
        for i in range(4):
            for h in range(2):
                at = rows(orders[h][i])
                columns = pl.ds(h * HALF, HALF)
                sent_o[2, h, at, :] = product(
                    (o_hi[at, columns], o_lo[at, columns]), (edge_hi[h], edge_lo[h])
                )
                last_copy(h, orders[h][i]).start()

    def last_rows(chunk):
        at = rows(chunk)
        for h in range(2):
            last_copy(1 - h, chunk).wait_recv()
            columns = pl.ds(h * HALF, HALF)
            o_hi[at, columns], o_lo[at, columns] = split(
                part_o[at, columns] + halo_o[2, h, at, :]
            )
        return product((o_hi[at, :], o_lo[at, :]), (c_hi[...], c_lo[...]))

    def mid_o():
        for h in range(2):
            at = pl.ds(h * HALF, HALF)
            part_o[:, at] = product((o_hi[...], o_lo[...]), (mid_hi[:, at], mid_lo[:, at]))

    def mid_c():
        for h in range(2):
            at = pl.ds(h * HALF, HALF)
            part_c[:, at] = product((mid_hi[...], mid_lo[...]), (c_hi[:, at], c_lo[:, at]))

    def next_c(k):
        for h in range(2):
            c_copies[k][1 - h].wait_recv()
            at = pl.ds(h * HALF, HALF)
            value = part_c[at, :] + product((edge_hi[h], edge_lo[h]), split(halo_c[k, h]))
            if k < 2:
                sent_c[k, at, :] = value
                c_copies[k + 1][h].start()
            c_hi[at, :], c_lo[at, :] = split(value)

    def next_o(k):
        for h in range(2):
            o_copies[k][1 - h].wait_recv()
            at = pl.ds(h * HALF, HALF)
            o_hi[:, at], o_lo[:, at] = split(part_o[:, at] + halo_o[k, h])

    def a_copy(k, z):
        at = pl.ds(z * TILE, TILE)
        return remote(
            sent_a.at[k, at], got_a.at[k, at], a_send.at[k, z], a_recv.at[k, z], partner
        )

    def block(k):
        def rows_of(which):
            at = pl.ds(pl.multiple_of(which * HALF, HALF), HALF)
            return product((o_hi[at, :], o_lo[at, :]), (c_hi[...], c_lo[...]))

        sent_a[k] = rows_of(1 - core)
        for z in range(2):
            a_copy(k, z).start()
        own[...] = rows_of(core)

    def over_x(k):
        for z in range(2):
            a_copy(k, z).wait_recv()
        sent_x[k] = (own[...] + got_a[k]).reshape(2, 4, 2 * PIECE, COLS)

        def send(d, carry):
            xd = lax.rem(x + d, 4)
            remote(
                sent_x.at[k, :, xd],
                got_x.at[k, 3 - d],
                x_send.at[k],
                x_recv.at[k],
                (xd * 4 + z_hi * 2 + core, col),
            ).start()
            return carry

        lax.fori_loop(1, 4, send, 0)

    z_ring = z_hi * 2 + z_lo
    z_way = 2 * y_hi - 1
    z_next = lax.rem(z_ring + z_way + 4, 4)
    z_after = (x * 4 + lax.div(z_next, 2) * 2 + core, lax.rem(z_next, 2) * 4 + y)

    def z_piece(k, which):
        at = pl.ds(pl.multiple_of(lax.rem(which, 2) * PIECE, PIECE), PIECE)
        return sent_z.at[k, lax.div(which, 2), at]

    def ring_copy(k, t):
        which = lax.rem(z_ring - (t + 1) * z_way + 8, 4)
        source = ring_z.at[k, t - 1] if t else z_piece(k, which)
        return remote(source, got_z.at[k, t], z_send.at[k, t], z_recv.at[k, t], z_after)

    def ring(k, t):
        which = lax.rem(z_ring - (t + 1) * z_way + 8, 4)
        ring_copy(k, t - 1).wait_recv()
        ring_z[k, t - 1] = z_piece(k, which)[...] + got_z[k, t - 1]
        ring_copy(k, t).start()

    def over_z(k):
        wait_all(got_x.at[k], x_recv.at[k])
        sent_z[k] = sent_x[k, :, x] + got_x[k, 0] + got_x[k, 1] + got_x[k, 2]
        if k < 4:
            ring_copy(k, 0).start()
            return

        def send(d, carry):
            there = lax.rem(z_hi * 2 + z_lo + d, 4)
            zhd, zld = lax.div(there, 2), lax.rem(there, 2)
            remote(
                sent_z.at[k, zhd, pl.ds(pl.multiple_of(zld * PIECE, PIECE), PIECE)],
                got_z.at[k, 3 - d],
                z_send.at[k, 0],
                z_recv.at[k, 0],
                (x * 4 + zhd * 2 + core, zld * 4 + y),
            ).start()
            return carry

        lax.fori_loop(1, 4, send, 0)

    def send_y(k, total):
        sent_y[k, 0] = total[:, :HALF]
        sent_y[k, 1] = total[:, HALF:]

        def send(d, carry):
            device, half = along_y(d)
            remote(
                sent_y.at[k, half], got_y.at[k, 3 - d], y_send.at[k], y_recv.at[k], device
            ).start()
            return carry

        lax.fori_loop(1, 4, send, 0)

    def over_y(k):
        total = z_piece(k, z_ring)[...]
        if k < 4:
            ring_copy(k, 2).wait_recv()
            send_y(k, total + got_z[k, 2])
        else:
            wait_all(got_z.at[k], z_recv.at[k, 0])
            send_y(k, total + got_z[k, 0] + got_z[k, 1] + got_z[k, 2])

    def last_plane(z):
        same = z_hi if z else 1 - z_hi

        def send(d, carry):
            there = lax.rem(mine + d, 8)
            xd, zld = lax.div(there, 2), lax.rem(there, 2)

            @pl.when(d + 1 - same > 0)
            def _():
                remote(
                    sent_x.at[6, z, xd, pl.ds(pl.multiple_of(zld * PIECE, PIECE), PIECE)],
                    got_p.at[7 + d * (1 - 2 * same)],
                    p_sems.at[0],
                    p_sems.at[1],
                    (xd * 4 + z * 2 + core, zld * 4 + y),
                ).start()

            return carry

        lax.fori_loop(0, 8, send, 0)

    def last_over_y():
        wait_all(got_p, p_sems.at[1])
        total = sent_x[6, z_hi, x, pl.ds(pl.multiple_of(z_lo * PIECE, PIECE), PIECE), :]
        for i in range(15):
            total = total + got_p[i]
        send_y(6, total)

    def finish(k):
        wait_all(got_y.at[k], y_recv.at[k])
        total = sent_y[k, lax.rem(y, 2)] + got_y[k, 0] + got_y[k, 1] + got_y[k, 2]
        done[k] = total * (1.0 / math.sqrt(ORDER))

    def send_done(first, last):
        def send(d, carry):
            there = lax.rem(mine + d, 8)
            xd, zld = lax.div(there, 2), lax.rem(there, 2)
            wanted = xd + 2 * zld + y_hi

            @pl.when(jnp.logical_and(wanted >= first, wanted <= last))
            def _():
                remote(
                    done.at[wanted],
                    got_d.at[7 - d],
                    d_sems.at[0],
                    d_sems.at[1],
                    (xd * 4 + z_hi * 2 + core, zld * 4 + y),
                ).start()

            return carry

        lax.fori_loop(1, 8, send, 0)

    send_o(0)
    mid_o()
    block(0)
    mid_c()
    over_x(0)

    next_c(0)
    block(1)
    mid_c()
    over_x(1)
    over_z(0)

    next_o(0)
    send_o(1)
    block(2)
    mid_o()
    over_x(2)
    ring(0, 1)
    over_z(1)

    next_c(1)
    block(3)
    mid_c()
    over_x(3)
    ring(0, 2)
    ring(1, 1)
    over_z(2)

    next_o(1)
    send_last_o()
    block(4)
    mid_o()
    over_x(4)
    ring(1, 2)
    ring(2, 1)
    over_z(3)

    next_c(2)
    block(5)
    over_x(5)
    ring(2, 2)
    ring(3, 1)
    over_z(4)

    for z in range(2):
        sent_a[6, pl.ds(z * TILE, TILE), :] = last_rows((1 - core) * 2 + z)
        a_copy(6, z).start()
    ring(3, 2)
    for z in range(2):
        value = last_rows(core * 2 + z)
        a_copy(6, z).wait_recv()
        sent_x[6, z] = (value + got_a[6, pl.ds(z * TILE, TILE), :]).reshape(4, 2 * PIECE, COLS)
        last_plane(z)
    over_z(5)
    for k in range(5):
        over_y(k)
    for k in range(5):
        finish(k)
    send_done(0, 4)
    last_over_y()
    over_y(5)
    finish(6)
    finish(5)
    send_done(5, 6)

    out[pl.ds(pl.multiple_of(mine * PIECE, PIECE), PIECE), :] = done[x + 2 * z_lo + y_hi]
    wait_all(got_d, d_sems.at[1])
    for i in range(7):
        source = lax.rem(mine + 1 + i, 8)
        out[pl.ds(pl.multiple_of(source * PIECE, PIECE), PIECE), :] = got_d[i]

    wait_all(got_d, d_sems.at[0])
    for copies in c_copies + o_copies:
        for copy in copies:
            copy.wait_send()
    for chunk in range(4):
        for side in range(2):
            last_copy(side, chunk).wait_send()
    for k in range(BLOCKS):
        for z in range(2):
            a_copy(k, z).wait_send()
        wait_all(got_y.at[k], y_send.at[k])
        if k < 6:
            wait_all(got_x.at[k], x_send.at[k])
        if k < 4:
            for t in range(3):
                ring_copy(k, t).wait_send()
    for k in range(4, 6):
        wait_all(got_z.at[k], z_send.at[k, 0])
    wait_all(got_p, p_sems.at[0])


def local(ctrl_start, obsv_start, band_tiles, band_offsets):
    vmem, dma = pltpu.VMEM, pltpu.SemaphoreType.DMA
    return pl.pallas_call(
        kernel,
        out_shape=jax.ShapeDtypeStruct((TILE, HALF), F32),
        in_specs=[pl.BlockSpec(memory_space=pl.ANY)] * 3
        + [pl.BlockSpec(memory_space=pltpu.SMEM)],
        out_specs=pl.BlockSpec(memory_space=pltpu.VMEM),
        scratch_shapes=[
            vmem((ROWS, COLS), F32),
            vmem((ROWS, COLS), F32),
            vmem((ROWS, 3 * TILE), F32),
            vmem((3, 2, HALF, COLS), F32),
            vmem((3, 2, COLS, HALF), F32),
            vmem((2, ROWS, COLS), F32),
            vmem((3, 2, COLS, HALF), F32),
            vmem((ROWS, COLS), F32),
            vmem((COLS, ROWS), F32),
            vmem((ROWS, ROWS), BF16),
            vmem((ROWS, ROWS), BF16),
            vmem((2, HALF, HALF), BF16),
            vmem((2, HALF, HALF), BF16),
            vmem((ROWS, COLS), BF16),
            vmem((ROWS, COLS), BF16),
            vmem((COLS, ROWS), BF16),
            vmem((COLS, ROWS), BF16),
            vmem((BLOCKS, HALF, COLS), F32),
            vmem((HALF, COLS), F32),
            vmem((BLOCKS, HALF, COLS), F32),
            vmem((BLOCKS, 2, 4, 2 * PIECE, COLS), F32),
            vmem((6, 3, 2, 2 * PIECE, COLS), F32),
            vmem((6, 2, 2 * PIECE, COLS), F32),
            vmem((4, 2, PIECE, COLS), F32),
            vmem((6, 3, PIECE, COLS), F32),
            vmem((15, PIECE, COLS), F32),
            vmem((BLOCKS, 2, PIECE, HALF), F32),
            vmem((BLOCKS, 3, PIECE, HALF), F32),
            vmem((BLOCKS, PIECE, HALF), F32),
            vmem((7, PIECE, HALF), F32),
            dma((3,)),
            dma((3, 2)),
            dma((3, 2)),
            dma((2, 2)),
            dma((2, 2)),
            dma((2, 4)),
            dma((2, 4)),
            dma((BLOCKS, 2)),
            dma((BLOCKS, 2)),
            dma((6,)),
            dma((6,)),
            dma((6, 3)),
            dma((6, 3)),
            dma((2,)),
            dma((BLOCKS,)),
            dma((BLOCKS,)),
            dma((2,)),
        ],
        compiler_params=pltpu.CompilerParams(
            collective_id=0, has_side_effects=True, vmem_limit_bytes=60 * 1024 * 1024
        ),
    )(ctrl_start, obsv_start, band_tiles, band_offsets)


def solution(mesh):
    placed = P(("row", "col"), None)
    return jax.shard_map(
        local, mesh=mesh, in_specs=(placed,) * 4, out_specs=P("row", "col"), check_vma=False
    )
```

```python
import math

import jax
import jax.numpy as jnp
from jax import lax
from jax.experimental import pallas as pl
from jax.experimental.pallas import tpu as pltpu
from jax.sharding import PartitionSpec as P

TILE = 128
HALF = 256
ROWS = 512
COLS = 512
ORDER = 65536
BLOCKS = 7
PIECE = 16
MESH = pl.DeviceIdType.MESH
F32 = jnp.float32
BF16 = jnp.bfloat16


def split(value):
    high = value.astype(BF16)
    return high, (value - high.astype(F32)).astype(BF16)


def product(left, right):
    def dot(a, b):
        return jnp.dot(a, b, preferred_element_type=F32)

    return dot(left[0], right[0]) + (dot(left[0], right[1]) + dot(left[1], right[0]))


def kernel(
    ctrl_in, obsv_in, band_in, offsets, out, ctrl, obsv, band,
    halo_c, halo_o, sent_c, sent_o, part_c, part_o,
    mid_hi, mid_lo, edge_hi, edge_lo, c_hi, c_lo, o_hi, o_lo,
    sent_a, own, got_a, sent_x, got_x, sent_z, ring_z, got_z, got_p, sent_y, got_y, done, got_d,
    in_sems, hc_send, hc_recv, ho_send, ho_recv, last_send, last_recv, a_send, a_recv,
    x_send, x_recv, z_send, z_recv, p_sems, y_send, y_recv, d_sems,
):
    row, col = lax.axis_index("row"), lax.axis_index("col")
    shard = row * 8 + col
    core, z_hi, x = lax.rem(row, 2), lax.rem(lax.div(row, 2), 2), lax.div(row, 4)
    y, z_lo = lax.rem(col, 4), lax.div(col, 4)
    place = x * 4 + z_hi * 2 + z_lo
    mine = x * 2 + z_lo
    y_hi = lax.div(y, 2)
    before, after = lax.rem(shard + 127, 128), lax.rem(shard + 1, 128)
    before = (lax.div(before, 8), lax.rem(before, 8))
    after = (lax.div(after, 8), lax.rem(after, 8))
    partner = (row + 1 - 2 * core, col)

    def in_plane(d):
        there = lax.rem(place + d, 16)
        xd, zhd, zld = lax.div(there, 4), lax.rem(lax.div(there, 2), 2), lax.rem(there, 2)
        return xd * 4 + zhd * 2 + core, zld * 4 + y

    def along_y(d):
        yd = lax.rem(y + d, 4)
        return (row, z_lo * 4 + yd), lax.rem(yd, 2)

    barrier = pltpu.get_barrier_semaphore()
    for device in (before, after, partner):
        pl.semaphore_signal(barrier, inc=1, device_id=device, device_id_type=MESH)

    def greet_plane(d, carry):
        pl.semaphore_signal(barrier, inc=1, device_id=in_plane(d), device_id_type=MESH)
        return carry

    def greet_y(d, carry):
        pl.semaphore_signal(barrier, inc=1, device_id=along_y(d)[0], device_id_type=MESH)
        return carry

    lax.fori_loop(1, 16, greet_plane, 0)
    lax.fori_loop(1, 4, greet_y, 0)
    inputs = [
        pltpu.make_async_copy(source, target, in_sems.at[i])
        for i, (source, target) in enumerate(((band_in, band), (obsv_in, obsv), (ctrl_in, ctrl)))
    ]
    for copy in inputs:
        copy.start()
    pl.semaphore_wait(barrier, 21)

    def remote(source, target, send, recv, device):
        return pltpu.make_async_remote_copy(
            src_ref=source,
            dst_ref=target,
            send_sem=send,
            recv_sem=recv,
            device_id=device,
            device_id_type=MESH,
        )

    def exchange(halves, halo, send, recv, k):
        copies = (
            remote(halves[0], halo.at[k, 1], send.at[k, 0], recv.at[k, 1], before),
            remote(halves[1], halo.at[k, 0], send.at[k, 1], recv.at[k, 0], after),
        )
        return copies

    def wait_all(ref, semaphore):
        pltpu.make_async_copy(ref, ref, semaphore).wait()

    c_copies = [
        exchange((src.at[pl.ds(0, HALF)], src.at[pl.ds(HALF, HALF)]), halo_c, hc_send, hc_recv, k)
        for k, src in enumerate((ctrl_in, sent_c.at[0], sent_c.at[1]))
    ]
    o_copies = [
        exchange((sent_o.at[k, 0], sent_o.at[k, 1]), halo_o, ho_send, ho_recv, k)
        for k in range(2)
    ]

    def last_copy(side, chunk):
        return remote(
            sent_o.at[2, side, pl.ds(pl.multiple_of(chunk * TILE, TILE), TILE)],
            halo_o.at[2, 1 - side, pl.ds(pl.multiple_of(chunk * TILE, TILE), TILE)],
            last_send.at[side, chunk],
            last_recv.at[1 - side, chunk],
            (before, after)[side],
        )

    for copy in c_copies[0]:
        copy.start()

    inputs[0].wait()
    mid_hi[...] = jnp.zeros_like(mid_hi)
    mid_lo[...] = jnp.zeros_like(mid_lo)
    edge_hi[...] = jnp.zeros_like(edge_hi)
    edge_lo[...] = jnp.zeros_like(edge_lo)
    no_before = 1 - lax.min(shard, 1)
    no_after = lax.div(shard, 127)
    for t in range(4):
        tiles = [band[pl.ds(t * TILE, TILE), pl.ds(b * TILE, TILE)] for b in range(3)]
        for o in range(5):
            e = t + o
            tile = jnp.zeros((TILE, TILE), F32)
            for b in range(3):
                given = offsets[t, b]
                if e < 2:
                    given = given + 100 * no_before
                if e >= 6:
                    given = given + 100 * no_after
                tile = jnp.where(jnp.full((TILE, TILE), given, jnp.int32) == o - 2, tiles[b], tile)
            high, low = split(tile)
            if e < 2:
                to_hi, to_lo, r, c = edge_hi.at[0], edge_lo.at[0], t, e
            elif e < 6:
                to_hi, to_lo, r, c = mid_hi, mid_lo, t, e - 2
            else:
                to_hi, to_lo, r, c = edge_hi.at[1], edge_lo.at[1], t - 2, e - 6
            to_hi[pl.ds(r * TILE, TILE), pl.ds(c * TILE, TILE)] = high
            to_lo[pl.ds(r * TILE, TILE), pl.ds(c * TILE, TILE)] = low

    inputs[1].wait()
    for q in range(4):
        high, low = split(obsv[:, pl.ds(q * TILE, TILE)].T)
        at = pl.ds((q % 2) * HALF + (q // 2) * TILE, TILE)
        o_hi[at, :] = high
        o_lo[at, :] = low
    inputs[2].wait()
    c_hi[...], c_lo[...] = split(ctrl[...])

    def send_o(k):
        for h in range(2):
            at = pl.ds(h * HALF, HALF)
            sent_o[k, h] = product((o_hi[:, at], o_lo[:, at]), (edge_hi[h], edge_lo[h]))
            o_copies[k][h].start()

    def chunks_for(its_core):
        return [(1 - its_core) * 2, (1 - its_core) * 2 + 1, its_core * 2, its_core * 2 + 1]

    def rows(chunk):
        return pl.ds(pl.multiple_of(chunk * TILE, TILE), TILE)

    def send_last_o():
        orders = [chunks_for(lax.rem(device[0], 2)) for device in (before, after)]
        for i in range(4):
            for h in range(2):
                at = rows(orders[h][i])
                columns = pl.ds(h * HALF, HALF)
                sent_o[2, h, at, :] = product(
                    (o_hi[at, columns], o_lo[at, columns]), (edge_hi[h], edge_lo[h])
                )
                last_copy(h, orders[h][i]).start()

    def last_rows(chunk):
        at = rows(chunk)
        for h in range(2):
            last_copy(1 - h, chunk).wait_recv()
            columns = pl.ds(h * HALF, HALF)
            o_hi[at, columns], o_lo[at, columns] = split(
                part_o[at, columns] + halo_o[2, h, at, :]
            )
        return product((o_hi[at, :], o_lo[at, :]), (c_hi[...], c_lo[...]))

    def mid_o():
        for h in range(2):
            at = pl.ds(h * HALF, HALF)
            part_o[:, at] = product((o_hi[...], o_lo[...]), (mid_hi[:, at], mid_lo[:, at]))

    def mid_c():
        for h in range(2):
            at = pl.ds(h * HALF, HALF)
            part_c[:, at] = product((mid_hi[...], mid_lo[...]), (c_hi[:, at], c_lo[:, at]))

    def next_c(k):
        for h in range(2):
            c_copies[k][1 - h].wait_recv()
            at = pl.ds(h * HALF, HALF)
            value = part_c[at, :] + product((edge_hi[h], edge_lo[h]), split(halo_c[k, h]))
            if k < 2:
                sent_c[k, at, :] = value
                c_copies[k + 1][h].start()
            c_hi[at, :], c_lo[at, :] = split(value)

    def next_o(k):
        for h in range(2):
            o_copies[k][1 - h].wait_recv()
            at = pl.ds(h * HALF, HALF)
            o_hi[:, at], o_lo[:, at] = split(part_o[:, at] + halo_o[k, h])

    def a_copy(k, z):
        at = pl.ds(z * TILE, TILE)
        return remote(
            sent_a.at[k, at], got_a.at[k, at], a_send.at[k, z], a_recv.at[k, z], partner
        )

    def block(k):
        def rows_of(which):
            at = pl.ds(pl.multiple_of(which * HALF, HALF), HALF)
            return product((o_hi[at, :], o_lo[at, :]), (c_hi[...], c_lo[...]))

        sent_a[k] = rows_of(1 - core)
        for z in range(2):
            a_copy(k, z).start()
        own[...] = rows_of(core)

    def over_x(k):
        for z in range(2):
            a_copy(k, z).wait_recv()
        sent_x[k] = (own[...] + got_a[k]).reshape(2, 4, 2 * PIECE, COLS)

        def send(d, carry):
            xd = lax.rem(x + d, 4)
            remote(
                sent_x.at[k, :, xd],
                got_x.at[k, 3 - d],
                x_send.at[k],
                x_recv.at[k],
                (xd * 4 + z_hi * 2 + core, col),
            ).start()
            return carry

        lax.fori_loop(1, 4, send, 0)

    z_ring = z_hi * 2 + z_lo
    z_way = 2 * y_hi - 1
    z_next = lax.rem(z_ring + z_way + 4, 4)
    z_after = (x * 4 + lax.div(z_next, 2) * 2 + core, lax.rem(z_next, 2) * 4 + y)

    def z_piece(k, which):
        at = pl.ds(pl.multiple_of(lax.rem(which, 2) * PIECE, PIECE), PIECE)
        return sent_z.at[k, lax.div(which, 2), at]

    def ring_copy(k, t):
        which = lax.rem(z_ring - (t + 1) * z_way + 8, 4)
        source = ring_z.at[k, t - 1] if t else z_piece(k, which)
        return remote(source, got_z.at[k, t], z_send.at[k, t], z_recv.at[k, t], z_after)

    def ring(k, t):
        which = lax.rem(z_ring - (t + 1) * z_way + 8, 4)
        ring_copy(k, t - 1).wait_recv()
        ring_z[k, t - 1] = z_piece(k, which)[...] + got_z[k, t - 1]
        ring_copy(k, t).start()

    def over_z(k):
        wait_all(got_x.at[k], x_recv.at[k])
        sent_z[k] = sent_x[k, :, x] + got_x[k, 0] + got_x[k, 1] + got_x[k, 2]
        if k < 4:
            ring_copy(k, 0).start()
            return

        def send(d, carry):
            there = lax.rem(z_hi * 2 + z_lo + d, 4)
            zhd, zld = lax.div(there, 2), lax.rem(there, 2)
            remote(
                sent_z.at[k, zhd, pl.ds(pl.multiple_of(zld * PIECE, PIECE), PIECE)],
                got_z.at[k, 3 - d],
                z_send.at[k, 0],
                z_recv.at[k, 0],
                (x * 4 + zhd * 2 + core, zld * 4 + y),
            ).start()
            return carry

        lax.fori_loop(1, 4, send, 0)

    def send_y(k, total):
        sent_y[k, 0] = total[:, :HALF]
        sent_y[k, 1] = total[:, HALF:]

        def send(d, carry):
            device, half = along_y(d)
            remote(
                sent_y.at[k, half], got_y.at[k, 3 - d], y_send.at[k], y_recv.at[k], device
            ).start()
            return carry

        lax.fori_loop(1, 4, send, 0)

    def over_y(k):
        total = z_piece(k, z_ring)[...]
        if k < 4:
            ring_copy(k, 2).wait_recv()
            send_y(k, total + got_z[k, 2])
        else:
            wait_all(got_z.at[k], z_recv.at[k, 0])
            send_y(k, total + got_z[k, 0] + got_z[k, 1] + got_z[k, 2])

    def last_plane(z):
        same = z_hi if z else 1 - z_hi

        def send(d, carry):
            there = lax.rem(mine + d, 8)
            xd, zld = lax.div(there, 2), lax.rem(there, 2)

            @pl.when(d + 1 - same > 0)
            def _():
                remote(
                    sent_x.at[6, z, xd, pl.ds(pl.multiple_of(zld * PIECE, PIECE), PIECE)],
                    got_p.at[7 + d * (1 - 2 * same)],
                    p_sems.at[0],
                    p_sems.at[1],
                    (xd * 4 + z * 2 + core, zld * 4 + y),
                ).start()

            return carry

        lax.fori_loop(0, 8, send, 0)

    def last_over_y():
        wait_all(got_p, p_sems.at[1])
        total = sent_x[6, z_hi, x, pl.ds(pl.multiple_of(z_lo * PIECE, PIECE), PIECE), :]
        for i in range(15):
            total = total + got_p[i]
        send_y(6, total)

    def finish(k):
        wait_all(got_y.at[k], y_recv.at[k])
        total = sent_y[k, lax.rem(y, 2)] + got_y[k, 0] + got_y[k, 1] + got_y[k, 2]
        done[k] = total * (1.0 / math.sqrt(ORDER))

    def send_done(first, last):
        def send(d, carry):
            there = lax.rem(mine + d, 8)
            xd, zld = lax.div(there, 2), lax.rem(there, 2)
            wanted = xd + 2 * zld + y_hi

            @pl.when(jnp.logical_and(wanted >= first, wanted <= last))
            def _():
                remote(
                    done.at[wanted],
                    got_d.at[7 - d],
                    d_sems.at[0],
                    d_sems.at[1],
                    (xd * 4 + z_hi * 2 + core, zld * 4 + y),
                ).start()

            return carry

        lax.fori_loop(1, 8, send, 0)

    send_o(0)
    mid_o()
    block(0)
    mid_c()
    over_x(0)

    next_c(0)
    block(1)
    mid_c()
    over_x(1)
    over_z(0)

    next_o(0)
    send_o(1)
    block(2)
    mid_o()
    over_x(2)
    ring(0, 1)
    over_z(1)

    next_c(1)
    block(3)
    mid_c()
    over_x(3)
    ring(0, 2)
    ring(1, 1)
    over_z(2)

    next_o(1)
    send_last_o()
    block(4)
    mid_o()
    over_x(4)
    ring(1, 2)
    ring(2, 1)
    over_z(3)

    next_c(2)
    block(5)
    over_x(5)
    ring(2, 2)
    ring(3, 1)
    over_z(4)

    for z in range(2):
        sent_a[6, pl.ds(z * TILE, TILE), :] = last_rows((1 - core) * 2 + z)
        a_copy(6, z).start()
    ring(3, 2)
    for z in range(2):
        value = last_rows(core * 2 + z)
        a_copy(6, z).wait_recv()
        sent_x[6, z] = (value + got_a[6, pl.ds(z * TILE, TILE), :]).reshape(4, 2 * PIECE, COLS)
        last_plane(z)
    over_z(5)
    for k in range(5):
        over_y(k)
    last_over_y()
    over_y(5)
    for k in range(5):
        finish(k)
    send_done(0, 4)
    finish(6)
    finish(5)
    send_done(5, 6)

    out[pl.ds(pl.multiple_of(mine * PIECE, PIECE), PIECE), :] = done[x + 2 * z_lo + y_hi]
    wait_all(got_d, d_sems.at[1])
    for i in range(7):
        source = lax.rem(mine + 1 + i, 8)
        out[pl.ds(pl.multiple_of(source * PIECE, PIECE), PIECE), :] = got_d[i]

    wait_all(got_d, d_sems.at[0])
    for copies in c_copies + o_copies:
        for copy in copies:
            copy.wait_send()
    for chunk in range(4):
        for side in range(2):
            last_copy(side, chunk).wait_send()
    for k in range(BLOCKS):
        for z in range(2):
            a_copy(k, z).wait_send()
        wait_all(got_y.at[k], y_send.at[k])
        if k < 6:
            wait_all(got_x.at[k], x_send.at[k])
        if k < 4:
            for t in range(3):
                ring_copy(k, t).wait_send()
    for k in range(4, 6):
        wait_all(got_z.at[k], z_send.at[k, 0])
    wait_all(got_p, p_sems.at[0])


def local(ctrl_start, obsv_start, band_tiles, band_offsets):
    vmem, dma = pltpu.VMEM, pltpu.SemaphoreType.DMA
    return pl.pallas_call(
        kernel,
        out_shape=jax.ShapeDtypeStruct((TILE, HALF), F32),
        in_specs=[pl.BlockSpec(memory_space=pl.ANY)] * 3
        + [pl.BlockSpec(memory_space=pltpu.SMEM)],
        out_specs=pl.BlockSpec(memory_space=pltpu.VMEM),
        scratch_shapes=[
            vmem((ROWS, COLS), F32),
            vmem((ROWS, COLS), F32),
            vmem((ROWS, 3 * TILE), F32),
            vmem((3, 2, HALF, COLS), F32),
            vmem((3, 2, COLS, HALF), F32),
            vmem((2, ROWS, COLS), F32),
            vmem((3, 2, COLS, HALF), F32),
            vmem((ROWS, COLS), F32),
            vmem((COLS, ROWS), F32),
            vmem((ROWS, ROWS), BF16),
            vmem((ROWS, ROWS), BF16),
            vmem((2, HALF, HALF), BF16),
            vmem((2, HALF, HALF), BF16),
            vmem((ROWS, COLS), BF16),
            vmem((ROWS, COLS), BF16),
            vmem((COLS, ROWS), BF16),
            vmem((COLS, ROWS), BF16),
            vmem((BLOCKS, HALF, COLS), F32),
            vmem((HALF, COLS), F32),
            vmem((BLOCKS, HALF, COLS), F32),
            vmem((BLOCKS, 2, 4, 2 * PIECE, COLS), F32),
            vmem((6, 3, 2, 2 * PIECE, COLS), F32),
            vmem((6, 2, 2 * PIECE, COLS), F32),
            vmem((4, 2, PIECE, COLS), F32),
            vmem((6, 3, PIECE, COLS), F32),
            vmem((15, PIECE, COLS), F32),
            vmem((BLOCKS, 2, PIECE, HALF), F32),
            vmem((BLOCKS, 3, PIECE, HALF), F32),
            vmem((BLOCKS, PIECE, HALF), F32),
            vmem((7, PIECE, HALF), F32),
            dma((3,)),
            dma((3, 2)),
            dma((3, 2)),
            dma((2, 2)),
            dma((2, 2)),
            dma((2, 4)),
            dma((2, 4)),
            dma((BLOCKS, 2)),
            dma((BLOCKS, 2)),
            dma((6,)),
            dma((6,)),
            dma((6, 3)),
            dma((6, 3)),
            dma((2,)),
            dma((BLOCKS,)),
            dma((BLOCKS,)),
            dma((2,)),
        ],
        compiler_params=pltpu.CompilerParams(
            collective_id=0, has_side_effects=True, vmem_limit_bytes=60 * 1024 * 1024
        ),
    )(ctrl_start, obsv_start, band_tiles, band_offsets)


def solution(mesh):
    placed = P(("row", "col"), None)
    return jax.shard_map(
        local, mesh=mesh, in_specs=(placed,) * 4, out_specs=P("row", "col"), check_vma=False
    )
```

```python
import math

import jax
import jax.numpy as jnp
from jax import lax
from jax.experimental import pallas as pl
from jax.experimental.pallas import tpu as pltpu
from jax.sharding import PartitionSpec as P

TILE = 128
HALF = 256
ROWS = 512
COLS = 512
ORDER = 65536
BLOCKS = 7
PIECE = 16
MESH = pl.DeviceIdType.MESH
F32 = jnp.float32
BF16 = jnp.bfloat16


def split(value):
    high = value.astype(BF16)
    return high, (value - high.astype(F32)).astype(BF16)


def product(left, right):
    def dot(a, b):
        return jnp.dot(a, b, preferred_element_type=F32)

    return dot(left[0], right[0]) + (dot(left[0], right[1]) + dot(left[1], right[0]))


def kernel(
    ctrl_in, obsv_in, band_in, offsets, out, ctrl, obsv, band,
    halo_c, halo_o, sent_c, sent_o, part_c, part_o,
    mid_hi, mid_lo, edge_hi, edge_lo, c_hi, c_lo, o_hi, o_lo,
    sent_a, own, got_a, sent_x, got_x, sent_z, ring_z, got_z, got_p, sent_y, got_y, done, got_d,
    in_sems, hc_send, hc_recv, ho_send, ho_recv, last_send, last_recv, a_send, a_recv,
    x_send, x_recv, z_send, z_recv, p_sems, y_send, y_recv, d_sems,
):
    row, col = lax.axis_index("row"), lax.axis_index("col")
    shard = row * 8 + col
    core, z_hi, x = lax.rem(row, 2), lax.rem(lax.div(row, 2), 2), lax.div(row, 4)
    y, z_lo = lax.rem(col, 4), lax.div(col, 4)
    place = x * 4 + z_hi * 2 + z_lo
    mine = x * 2 + z_lo
    y_hi = lax.div(y, 2)
    before, after = lax.rem(shard + 127, 128), lax.rem(shard + 1, 128)
    before = (lax.div(before, 8), lax.rem(before, 8))
    after = (lax.div(after, 8), lax.rem(after, 8))
    partner = (row + 1 - 2 * core, col)

    def in_plane(d):
        there = lax.rem(place + d, 16)
        xd, zhd, zld = lax.div(there, 4), lax.rem(lax.div(there, 2), 2), lax.rem(there, 2)
        return xd * 4 + zhd * 2 + core, zld * 4 + y

    def along_y(d):
        yd = lax.rem(y + d, 4)
        return (row, z_lo * 4 + yd), lax.rem(yd, 2)

    barrier = pltpu.get_barrier_semaphore()
    for device in (before, after, partner):
        pl.semaphore_signal(barrier, inc=1, device_id=device, device_id_type=MESH)

    def greet_plane(d, carry):
        pl.semaphore_signal(barrier, inc=1, device_id=in_plane(d), device_id_type=MESH)
        return carry

    def greet_y(d, carry):
        pl.semaphore_signal(barrier, inc=1, device_id=along_y(d)[0], device_id_type=MESH)
        return carry

    lax.fori_loop(1, 16, greet_plane, 0)
    lax.fori_loop(1, 4, greet_y, 0)
    inputs = [
        pltpu.make_async_copy(source, target, in_sems.at[i])
        for i, (source, target) in enumerate(((band_in, band), (obsv_in, obsv), (ctrl_in, ctrl)))
    ]
    for copy in inputs:
        copy.start()
    pl.semaphore_wait(barrier, 21)

    def remote(source, target, send, recv, device):
        return pltpu.make_async_remote_copy(
            src_ref=source,
            dst_ref=target,
            send_sem=send,
            recv_sem=recv,
            device_id=device,
            device_id_type=MESH,
        )

    def exchange(halves, halo, send, recv, k):
        copies = (
            remote(halves[0], halo.at[k, 1], send.at[k, 0], recv.at[k, 1], before),
            remote(halves[1], halo.at[k, 0], send.at[k, 1], recv.at[k, 0], after),
        )
        return copies

    def wait_all(ref, semaphore):
        pltpu.make_async_copy(ref, ref, semaphore).wait()

    c_copies = [
        exchange((src.at[pl.ds(0, HALF)], src.at[pl.ds(HALF, HALF)]), halo_c, hc_send, hc_recv, k)
        for k, src in enumerate((ctrl_in, sent_c.at[0], sent_c.at[1]))
    ]
    o_copies = [
        exchange((sent_o.at[k, 0], sent_o.at[k, 1]), halo_o, ho_send, ho_recv, k)
        for k in range(2)
    ]

    def last_copy(side, chunk):
        return remote(
            sent_o.at[2, side, pl.ds(pl.multiple_of(chunk * TILE, TILE), TILE)],
            halo_o.at[2, 1 - side, pl.ds(pl.multiple_of(chunk * TILE, TILE), TILE)],
            last_send.at[side, chunk],
            last_recv.at[1 - side, chunk],
            (before, after)[side],
        )

    for copy in c_copies[0]:
        copy.start()

    inputs[0].wait()
    mid_hi[...] = jnp.zeros_like(mid_hi)
    mid_lo[...] = jnp.zeros_like(mid_lo)
    edge_hi[...] = jnp.zeros_like(edge_hi)
    edge_lo[...] = jnp.zeros_like(edge_lo)
    no_before = 1 - lax.min(shard, 1)
    no_after = lax.div(shard, 127)
    for t in range(4):
        tiles = [band[pl.ds(t * TILE, TILE), pl.ds(b * TILE, TILE)] for b in range(3)]
        for o in range(5):
            e = t + o
            tile = jnp.zeros((TILE, TILE), F32)
            for b in range(3):
                given = offsets[t, b]
                if e < 2:
                    given = given + 100 * no_before
                if e >= 6:
                    given = given + 100 * no_after
                tile = jnp.where(jnp.full((TILE, TILE), given, jnp.int32) == o - 2, tiles[b], tile)
            high, low = split(tile)
            if e < 2:
                to_hi, to_lo, r, c = edge_hi.at[0], edge_lo.at[0], t, e
            elif e < 6:
                to_hi, to_lo, r, c = mid_hi, mid_lo, t, e - 2
            else:
                to_hi, to_lo, r, c = edge_hi.at[1], edge_lo.at[1], t - 2, e - 6
            to_hi[pl.ds(r * TILE, TILE), pl.ds(c * TILE, TILE)] = high
            to_lo[pl.ds(r * TILE, TILE), pl.ds(c * TILE, TILE)] = low

    inputs[1].wait()
    for q in range(4):
        high, low = split(obsv[:, pl.ds(q * TILE, TILE)].T)
        at = pl.ds((q % 2) * HALF + (q // 2) * TILE, TILE)
        o_hi[at, :] = high
        o_lo[at, :] = low
    inputs[2].wait()
    c_hi[...], c_lo[...] = split(ctrl[...])

    def send_o(k):
        for h in range(2):
            at = pl.ds(h * HALF, HALF)
            sent_o[k, h] = product((o_hi[:, at], o_lo[:, at]), (edge_hi[h], edge_lo[h]))
            o_copies[k][h].start()

    def chunks_for(its_core):
        return [(1 - its_core) * 2, (1 - its_core) * 2 + 1, its_core * 2, its_core * 2 + 1]

    def rows(chunk):
        return pl.ds(pl.multiple_of(chunk * TILE, TILE), TILE)

    def send_last_o():
        orders = [chunks_for(lax.rem(device[0], 2)) for device in (before, after)]
        for i in range(4):
            for h in range(2):
                at = rows(orders[h][i])
                columns = pl.ds(h * HALF, HALF)
                sent_o[2, h, at, :] = product(
                    (o_hi[at, columns], o_lo[at, columns]), (edge_hi[h], edge_lo[h])
                )
                last_copy(h, orders[h][i]).start()

    def last_rows(chunk):
        at = rows(chunk)
        for h in range(2):
            last_copy(1 - h, chunk).wait_recv()
            columns = pl.ds(h * HALF, HALF)
            o_hi[at, columns], o_lo[at, columns] = split(
                part_o[at, columns] + halo_o[2, h, at, :]
            )
        return product((o_hi[at, :], o_lo[at, :]), (c_hi[...], c_lo[...]))

    def mid_o():
        for h in range(2):
            at = pl.ds(h * HALF, HALF)
            part_o[:, at] = product((o_hi[...], o_lo[...]), (mid_hi[:, at], mid_lo[:, at]))

    def mid_c():
        for h in range(2):
            at = pl.ds(h * HALF, HALF)
            part_c[:, at] = product((mid_hi[...], mid_lo[...]), (c_hi[:, at], c_lo[:, at]))

    def next_c(k):
        for h in range(2):
            c_copies[k][1 - h].wait_recv()
            at = pl.ds(h * HALF, HALF)
            value = part_c[at, :] + product((edge_hi[h], edge_lo[h]), split(halo_c[k, h]))
            if k < 2:
                sent_c[k, at, :] = value
                c_copies[k + 1][h].start()
            c_hi[at, :], c_lo[at, :] = split(value)

    def next_o(k):
        for h in range(2):
            o_copies[k][1 - h].wait_recv()
            at = pl.ds(h * HALF, HALF)
            o_hi[:, at], o_lo[:, at] = split(part_o[:, at] + halo_o[k, h])

    def a_copy(k, z):
        at = pl.ds(z * TILE, TILE)
        return remote(
            sent_a.at[k, at], got_a.at[k, at], a_send.at[k, z], a_recv.at[k, z], partner
        )

    def block(k):
        def rows_of(which):
            at = pl.ds(pl.multiple_of(which * HALF, HALF), HALF)
            return product((o_hi[at, :], o_lo[at, :]), (c_hi[...], c_lo[...]))

        sent_a[k] = rows_of(1 - core)
        for z in range(2):
            a_copy(k, z).start()
        own[...] = rows_of(core)

    def over_x(k):
        for z in range(2):
            a_copy(k, z).wait_recv()
        sent_x[k] = (own[...] + got_a[k]).reshape(2, 4, 2 * PIECE, COLS)

        def send(d, carry):
            xd = lax.rem(x + d, 4)
            remote(
                sent_x.at[k, :, xd],
                got_x.at[k, 3 - d],
                x_send.at[k],
                x_recv.at[k],
                (xd * 4 + z_hi * 2 + core, col),
            ).start()
            return carry

        lax.fori_loop(1, 4, send, 0)

    z_ring = z_hi * 2 + z_lo
    z_way = 2 * y_hi - 1
    z_next = lax.rem(z_ring + z_way + 4, 4)
    z_after = (x * 4 + lax.div(z_next, 2) * 2 + core, lax.rem(z_next, 2) * 4 + y)

    def z_piece(k, which):
        at = pl.ds(pl.multiple_of(lax.rem(which, 2) * PIECE, PIECE), PIECE)
        return sent_z.at[k, lax.div(which, 2), at]

    def ring_copy(k, t):
        which = lax.rem(z_ring - (t + 1) * z_way + 8, 4)
        source = ring_z.at[k, t - 1] if t else z_piece(k, which)
        return remote(source, got_z.at[k, t], z_send.at[k, t], z_recv.at[k, t], z_after)

    def ring(k, t):
        which = lax.rem(z_ring - (t + 1) * z_way + 8, 4)
        ring_copy(k, t - 1).wait_recv()
        ring_z[k, t - 1] = z_piece(k, which)[...] + got_z[k, t - 1]
        ring_copy(k, t).start()

    def over_z(k):
        wait_all(got_x.at[k], x_recv.at[k])
        sent_z[k] = sent_x[k, :, x] + got_x[k, 0] + got_x[k, 1] + got_x[k, 2]
        if k < 4:
            ring_copy(k, 0).start()
            return

        def send(d, carry):
            there = lax.rem(z_hi * 2 + z_lo + d, 4)
            zhd, zld = lax.div(there, 2), lax.rem(there, 2)
            remote(
                sent_z.at[k, zhd, pl.ds(pl.multiple_of(zld * PIECE, PIECE), PIECE)],
                got_z.at[k, 3 - d],
                z_send.at[k, 0],
                z_recv.at[k, 0],
                (x * 4 + zhd * 2 + core, zld * 4 + y),
            ).start()
            return carry

        lax.fori_loop(1, 4, send, 0)

    def send_y(k, total):
        sent_y[k, 0] = total[:, :HALF]
        sent_y[k, 1] = total[:, HALF:]

        def send(d, carry):
            device, half = along_y(d)
            remote(
                sent_y.at[k, half], got_y.at[k, 3 - d], y_send.at[k], y_recv.at[k], device
            ).start()
            return carry

        lax.fori_loop(1, 4, send, 0)

    def over_y(k):
        total = z_piece(k, z_ring)[...]
        if k < 4:
            ring_copy(k, 2).wait_recv()
            send_y(k, total + got_z[k, 2])
        else:
            wait_all(got_z.at[k], z_recv.at[k, 0])
            send_y(k, total + got_z[k, 0] + got_z[k, 1] + got_z[k, 2])

    def last_plane(z):
        same = z_hi if z else 1 - z_hi

        def send(d, carry):
            there = lax.rem(mine + d, 8)
            xd, zld = lax.div(there, 2), lax.rem(there, 2)

            @pl.when(d + 1 - same > 0)
            def _():
                remote(
                    sent_x.at[6, z, xd, pl.ds(pl.multiple_of(zld * PIECE, PIECE), PIECE)],
                    got_p.at[7 + d * (1 - 2 * same)],
                    p_sems.at[0],
                    p_sems.at[1],
                    (xd * 4 + z * 2 + core, zld * 4 + y),
                ).start()

            return carry

        lax.fori_loop(0, 8, send, 0)

    def last_over_y():
        wait_all(got_p, p_sems.at[1])
        total = sent_x[6, z_hi, x, pl.ds(pl.multiple_of(z_lo * PIECE, PIECE), PIECE), :]
        for i in range(15):
            total = total + got_p[i]
        send_y(6, total)

    def finish(k):
        wait_all(got_y.at[k], y_recv.at[k])
        total = sent_y[k, lax.rem(y, 2)] + got_y[k, 0] + got_y[k, 1] + got_y[k, 2]
        done[k] = total * (1.0 / math.sqrt(ORDER))

    def send_done(first, last):
        def send(d, carry):
            there = lax.rem(mine + d, 8)
            xd, zld = lax.div(there, 2), lax.rem(there, 2)
            wanted = xd + 2 * zld + y_hi

            @pl.when(jnp.logical_and(wanted >= first, wanted <= last))
            def _():
                remote(
                    done.at[wanted],
                    got_d.at[7 - d],
                    d_sems.at[0],
                    d_sems.at[1],
                    (xd * 4 + z_hi * 2 + core, zld * 4 + y),
                ).start()

            return carry

        lax.fori_loop(1, 8, send, 0)

    send_o(0)
    mid_o()
    block(0)
    mid_c()
    over_x(0)

    next_c(0)
    block(1)
    mid_c()
    over_x(1)
    over_z(0)

    next_o(0)
    send_o(1)
    block(2)
    mid_o()
    over_x(2)
    ring(0, 1)
    over_z(1)

    next_c(1)
    block(3)
    mid_c()
    over_x(3)
    ring(0, 2)
    ring(1, 1)
    over_z(2)

    next_o(1)
    send_last_o()
    block(4)
    mid_o()
    over_x(4)
    ring(1, 2)
    ring(2, 1)
    over_z(3)

    next_c(2)
    block(5)
    over_x(5)
    ring(2, 2)
    ring(3, 1)
    over_z(4)

    for z in range(2):
        sent_a[6, pl.ds(z * TILE, TILE), :] = last_rows((1 - core) * 2 + z)
        a_copy(6, z).start()
    ring(3, 2)
    for k in range(3):
        over_y(k)
    for z in range(2):
        value = last_rows(core * 2 + z)
        a_copy(6, z).wait_recv()
        sent_x[6, z] = (value + got_a[6, pl.ds(z * TILE, TILE), :]).reshape(4, 2 * PIECE, COLS)
        last_plane(z)
    over_z(5)
    for k in range(3, 5):
        over_y(k)
    last_over_y()
    over_y(5)
    for k in range(5):
        finish(k)
    send_done(0, 4)
    finish(6)
    finish(5)
    send_done(5, 6)

    out[pl.ds(pl.multiple_of(mine * PIECE, PIECE), PIECE), :] = done[x + 2 * z_lo + y_hi]
    wait_all(got_d, d_sems.at[1])
    for i in range(7):
        source = lax.rem(mine + 1 + i, 8)
        out[pl.ds(pl.multiple_of(source * PIECE, PIECE), PIECE), :] = got_d[i]

    wait_all(got_d, d_sems.at[0])
    for copies in c_copies + o_copies:
        for copy in copies:
            copy.wait_send()
    for chunk in range(4):
        for side in range(2):
            last_copy(side, chunk).wait_send()
    for k in range(BLOCKS):
        for z in range(2):
            a_copy(k, z).wait_send()
        wait_all(got_y.at[k], y_send.at[k])
        if k < 6:
            wait_all(got_x.at[k], x_send.at[k])
        if k < 4:
            for t in range(3):
                ring_copy(k, t).wait_send()
    for k in range(4, 6):
        wait_all(got_z.at[k], z_send.at[k, 0])
    wait_all(got_p, p_sems.at[0])


def local(ctrl_start, obsv_start, band_tiles, band_offsets):
    vmem, dma = pltpu.VMEM, pltpu.SemaphoreType.DMA
    return pl.pallas_call(
        kernel,
        out_shape=jax.ShapeDtypeStruct((TILE, HALF), F32),
        in_specs=[pl.BlockSpec(memory_space=pl.ANY)] * 3
        + [pl.BlockSpec(memory_space=pltpu.SMEM)],
        out_specs=pl.BlockSpec(memory_space=pltpu.VMEM),
        scratch_shapes=[
            vmem((ROWS, COLS), F32),
            vmem((ROWS, COLS), F32),
            vmem((ROWS, 3 * TILE), F32),
            vmem((3, 2, HALF, COLS), F32),
            vmem((3, 2, COLS, HALF), F32),
            vmem((2, ROWS, COLS), F32),
            vmem((3, 2, COLS, HALF), F32),
            vmem((ROWS, COLS), F32),
            vmem((COLS, ROWS), F32),
            vmem((ROWS, ROWS), BF16),
            vmem((ROWS, ROWS), BF16),
            vmem((2, HALF, HALF), BF16),
            vmem((2, HALF, HALF), BF16),
            vmem((ROWS, COLS), BF16),
            vmem((ROWS, COLS), BF16),
            vmem((COLS, ROWS), BF16),
            vmem((COLS, ROWS), BF16),
            vmem((BLOCKS, HALF, COLS), F32),
            vmem((HALF, COLS), F32),
            vmem((BLOCKS, HALF, COLS), F32),
            vmem((BLOCKS, 2, 4, 2 * PIECE, COLS), F32),
            vmem((6, 3, 2, 2 * PIECE, COLS), F32),
            vmem((6, 2, 2 * PIECE, COLS), F32),
            vmem((4, 2, PIECE, COLS), F32),
            vmem((6, 3, PIECE, COLS), F32),
            vmem((15, PIECE, COLS), F32),
            vmem((BLOCKS, 2, PIECE, HALF), F32),
            vmem((BLOCKS, 3, PIECE, HALF), F32),
            vmem((BLOCKS, PIECE, HALF), F32),
            vmem((7, PIECE, HALF), F32),
            dma((3,)),
            dma((3, 2)),
            dma((3, 2)),
            dma((2, 2)),
            dma((2, 2)),
            dma((2, 4)),
            dma((2, 4)),
            dma((BLOCKS, 2)),
            dma((BLOCKS, 2)),
            dma((6,)),
            dma((6,)),
            dma((6, 3)),
            dma((6, 3)),
            dma((2,)),
            dma((BLOCKS,)),
            dma((BLOCKS,)),
            dma((2,)),
        ],
        compiler_params=pltpu.CompilerParams(
            collective_id=0, has_side_effects=True, vmem_limit_bytes=60 * 1024 * 1024
        ),
    )(ctrl_start, obsv_start, band_tiles, band_offsets)


def solution(mesh):
    placed = P(("row", "col"), None)
    return jax.shard_map(
        local, mesh=mesh, in_specs=(placed,) * 4, out_specs=P("row", "col"), check_vma=False
    )
```
